256 devices in a mesh: row: 64 (over y, z, core), col: 4 (over x).
Axes of the slice: x: 4, y: 4, z: 8, core: 2. Of those that a mesh axis runs over, the one named last changes fastest.
Arguments:
- fractions_source: float32 [12, 4096, 4096], P('col', 'row'), may hold values from 0 to 1, as said below
- x_source_edges: int32 [4097], replicated, may hold values from 0 to 196608, as said below
- x_target_edges: int32 [3073], replicated, may hold values from 0 to 196608, as said below
- y_source_edges: int32 [4097], replicated, may hold values from 0 to 196608, as said below
- y_target_edges: int32 [3073], replicated, may hold values from 0 to 196608, as said below
- conductivity_table: int32 [6], replicated, may hold values from 4 to 64
- capacity: float32 [6], replicated, may hold values from 0.5 to 4
- thermal_source_term: float32 [2, 3072, 3072], P(None, 'row', 'col'), may hold values from -40 to 40
Outputs:
- rezoned_occupancy_shares: float32 [12, 3072, 3072], P(None, 'row', 'col')
- thermal_iterate: float32 [2, 3072, 3072], P(None, 'row', 'col')
- remaining_defect: float32 [2, 3072, 3072], P(None, 'row', 'col')
The draws below stay inside these ranges and needn't reach their ends.
Inputs may be any that keep to these rules, and one draw needn't show every extreme that they name: `fractions_source`: positive; for every z layer and source cell the 6 materials' fractions sum to one. `x_source_edges`: strictly increasing; every 64-th source edge along x coincides with every 48-th target edge along x, at multiples of 3072; the first edge is 0 and the last is the largest value. `x_target_edges`: strictly increasing; shares the walls of x_source_edges at every 48-th edge; the first edge is 0 and the last is the largest value. `y_source_edges`: strictly increasing; every 64-th source edge along y coincides with every 48-th target edge along y, at multiples of 3072; the first edge is 0 and the last is the largest value. `y_target_edges`: strictly increasing; shares the walls of y_source_edges at every 48-th edge; the first edge is 0 and the last is the largest value.
All inputs are finite; a program needn't handle non-finite values.
Results may differ from the reference program's by a relative error of at most 0.0003.
Values sent between devices are 32-bit elements; how exact they have to be, the bound alone decides.
A program may use at most 64 MiB of HBM per device.

```python
import math
import jax
import jax.numpy as jnp
from jax import lax

M = 6
ZL = 2
SBLK = 64
TBLK = 48
ITERS = 3
NS = 4096
NT = 3072


def edge_draw(key, count_cells, spacing, wall_every, spread):
    offsets = jax.random.randint(key, (count_cells + 1,), -spread, spread + 1)
    positions = jnp.arange(count_cells + 1, dtype=jnp.int32)
    offsets = jnp.where(positions % wall_every == 0, 0, offsets)
    return (positions * spacing + offsets).astype(jnp.int32)


def draw_x_source_edges(key, part):
    return edge_draw(jax.random.fold_in(key, 11), NS, TBLK, SBLK, TBLK // 4)


def draw_x_target_edges(key, part):
    return edge_draw(jax.random.fold_in(key, 12), NT, SBLK, TBLK, SBLK // 4)


def draw_y_source_edges(key, part):
    return edge_draw(jax.random.fold_in(key, 13), NS, TBLK, SBLK, TBLK // 4)


def draw_y_target_edges(key, part):
    return edge_draw(jax.random.fold_in(key, 14), NT, SBLK, TBLK, SBLK // 4)


def draw_fractions_source(key, part):
    first_key = jax.random.fold_in(key, 21)
    weights_raw = jax.random.uniform(first_key, (ZL, M, NS, NS), jnp.float32, 0.05, 1.0)
    summed = jnp.sum(weights_raw, axis=1, keepdims=True)
    return (weights_raw / summed).reshape(ZL * M, NS, NS)


def draw_thermal_source_term(key, part):
    first_key = jax.random.fold_in(key, 31)
    ramp = jnp.arange(NT, dtype=jnp.float32) / (NT - 1)
    scaling = 10.0 ** (ramp[:, None] + ramp[None, :] - 1.0)
    return jax.random.truncated_normal(first_key, -4.0, 4.0, (ZL, NT, NT), jnp.float32) * scaling


def set_ends(entries, rng, smallest, top_value):
    index_at = [jax.random.randint(jax.random.fold_in(rng, axis), (), 0, length) for axis, length in enumerate(entries.shape)]
    longest = entries.shape.index(max(entries.shape))
    next_to = index_at[:longest] + [(index_at[longest] + 1) % entries.shape[longest]] + index_at[longest + 1:]
    return entries.at[tuple(index_at)].set(smallest).at[tuple(next_to)].set(top_value)


def setup_inputs(seed: int = 0) -> dict:
    arg_keys = jax.random.split(jax.random.key(seed), 9)
    fractions_source = draw_fractions_source(jax.random.fold_in(arg_keys[8], 71), 0)
    x_source_edges = draw_x_source_edges(jax.random.fold_in(arg_keys[8], 71), 0)
    x_target_edges = draw_x_target_edges(jax.random.fold_in(arg_keys[8], 71), 0)
    y_source_edges = draw_y_source_edges(jax.random.fold_in(arg_keys[8], 71), 0)
    y_target_edges = draw_y_target_edges(jax.random.fold_in(arg_keys[8], 71), 0)
    conductivity_table = set_ends(jax.random.randint(arg_keys[5], (M,), 4, 65), jax.random.fold_in(arg_keys[5], 1), 4, 64).astype(jnp.int32)
    capacity = jnp.clip(jnp.exp(jax.random.uniform(arg_keys[6], (M,), jnp.float32, math.log(0.5), math.log(4.0))), 0.5, 4.0)
    thermal_source_term = draw_thermal_source_term(jax.random.fold_in(arg_keys[8], 71), 0)
    return {"fractions_source": fractions_source, "x_source_edges": x_source_edges, "x_target_edges": x_target_edges, "y_source_edges": y_source_edges, "y_target_edges": y_target_edges, "conductivity_table": conductivity_table, "capacity": capacity, "thermal_source_term": thermal_source_term}


def margin_blocks(source_edges, target_mesh_edges, source_block, target_block):
    block_list = (source_edges.shape[0] - 1) // source_block
    src_lo = source_edges[:-1].reshape(block_list, 1, source_block)
    src_hi = source_edges[1:].reshape(block_list, 1, source_block)
    tgt_lo = target_mesh_edges[:-1].reshape(block_list, target_block, 1)
    tgt_hi = target_mesh_edges[1:].reshape(block_list, target_block, 1)
    shared = jnp.maximum(jnp.minimum(src_hi, tgt_hi) - jnp.maximum(src_lo, tgt_lo), 0)
    return shared.astype(jnp.float32) / (tgt_hi - tgt_lo).astype(jnp.float32)


def rezone_plane(layer_plane, weight_x, vertical_factor):
    block_list = weight_x.shape[0]
    target_block = weight_x.shape[1]
    source_block = weight_x.shape[2]
    source_grid = layer_plane.reshape(block_list, source_block, block_list, source_block)
    along_y = jnp.einsum("asbu,bvu->asbv", source_grid, vertical_factor, precision=lax.Precision.HIGHEST)
    along_x = jnp.einsum("asbv,ats->bvat", along_y, weight_x, precision=lax.Precision.HIGHEST)
    return along_x.reshape(block_list * target_block, block_list * target_block)


def face_weights(padded_array):
    center = padded_array[1:-1, 1:-1, 1:-1]
    neighbours = (padded_array[2:, 1:-1, 1:-1], padded_array[:-2, 1:-1, 1:-1], padded_array[1:-1, 2:, 1:-1],
                  padded_array[1:-1, :-2, 1:-1], padded_array[1:-1, 1:-1, 2:], padded_array[1:-1, 1:-1, :-2])
    return tuple(2.0 * center * beside / (center + beside) for beside in neighbours)


def stencil(padded_field, face_list, cell_capacity):
    center = padded_field[1:-1, 1:-1, 1:-1]
    neighbours = (padded_field[2:, 1:-1, 1:-1], padded_field[:-2, 1:-1, 1:-1], padded_field[1:-1, 2:, 1:-1],
                  padded_field[1:-1, :-2, 1:-1], padded_field[1:-1, 1:-1, 2:], padded_field[1:-1, 1:-1, :-2])
    result = cell_capacity * center
    for weight, beside in zip(face_list, neighbours):
        result = result + weight * (center - beside)
    return result


def reference(fractions_source, x_source_edges, x_target_edges, y_source_edges, y_target_edges, conductivity_table, capacity, thermal_source_term):
    weight_x = margin_blocks(x_source_edges, x_target_edges, SBLK, TBLK)
    vertical_factor = margin_blocks(y_source_edges, y_target_edges, SBLK, TBLK)
    rezoned_occupancy_shares = lax.map(lambda layer_plane: rezone_plane(layer_plane, weight_x, vertical_factor), fractions_source)
    stacked = rezoned_occupancy_shares.reshape(ZL, M, NT, NT)
    substance_diffusivity = conductivity_table.astype(jnp.float32) / 16.0
    inverse = jnp.sum(stacked / substance_diffusivity[None, :, None, None], axis=1)
    cell_k = 1.0 / inverse
    cell_capacity = jnp.sum(stacked * capacity[None, :, None, None], axis=1)
    face_list = face_weights(jnp.pad(cell_k, 1))
    thermal_iterate = jnp.zeros_like(thermal_source_term)
    remaining_defect = thermal_source_term
    conjugate_update_vector = thermal_source_term
    norm_now = jnp.sum(remaining_defect * remaining_defect)
    for iteration in range(ITERS):
        applied = stencil(jnp.pad(conjugate_update_vector, 1), face_list, cell_capacity)
        line_minimizer_alpha = norm_now / jnp.sum(conjugate_update_vector * applied)
        thermal_iterate = thermal_iterate + line_minimizer_alpha * conjugate_update_vector
        remaining_defect = remaining_defect - line_minimizer_alpha * applied
        norm_next = jnp.sum(remaining_defect * remaining_defect)
        conjugate_update_vector = remaining_defect + (norm_next / norm_now) * conjugate_update_vector
        norm_now = norm_next
    return rezoned_occupancy_shares, thermal_iterate, remaining_defect
```

```python
import jax
import jax.numpy as jnp
from jax import lax
from jax.experimental import pallas as pl
from jax.experimental.pallas import tpu as pltpu
from jax.sharding import PartitionSpec as P

M = 6
TB = 48
NQ = 32
LAG_FORWARD = 6
LAG_MERGE = 12
MESH = pl.DeviceIdType.MESH
F32 = jnp.float32
BF16 = jnp.bfloat16
VM = pltpu.VMEM
DMA = pltpu.SemaphoreType.DMA


def split(a):
    high = a.astype(BF16)
    return high, (a - high.astype(F32)).astype(BF16)


def product(ah, al, bh, bl, dims):
    def dot(p, q):
        return lax.dot_general(p, q, (dims, ((), ())), preferred_element_type=F32)

    return dot(ah, bh) + (dot(ah, bl) + dot(al, bh))


def offsets(k):
    g, s = k // 8, k % 2
    dz = jnp.where(s == 0, 4 - g, jnp.where(g == 0, 0, 4 + g))
    return (k // 2) % 4, dz


def lanes(shape):
    return lax.broadcasted_iota(jnp.int32, shape, len(shape) - 1)


def kernel(
    frac, src_rows, tgt_cols, param, b_ref, shares_out, x_out, r_out,
    fbuf, wxp, wah, wal, wbh, wbl, sbuf, rb1, rb2, R, bx, ix, v1, v2, v3, cc,
    fu, fd, fl, fr, fz, hs_row, hr_row, hs_col, hr_col, acc, tile_a, got_a, tile_b, got_b,
    fsem, ssem, rsem1, ssem2, rsem2, hs_sem, hr_sem, ts_sem, tr_sem, osem,
):
    r = lax.axis_index("row")
    c = lax.axis_index("col")
    core = r % 2
    chip = r // 2
    y, z = chip // 8, chip % 8
    half = c % 2

    def fetch(k):
        dy, dz = offsets(k)
        q = ((y + dy) % 4) * 8 + (z + dz) % 8
        return pltpu.make_async_copy(
            frac.at[:, :, pl.ds(pl.multiple_of(q * 128, 128), 128)], fbuf.at[k], fsem.at[k]
        )

    @pl.loop(0, NQ)
    def _(k):
        fetch(k).start()

    barrier = pltpu.get_barrier_semaphore()

    def greet(row, col):
        pl.semaphore_signal(barrier, inc=1, device_id=(row, col), device_id_type=MESH)

    @pl.loop(1, 64)
    def _(j):
        greet((r + j) % 64, c)

    @pl.loop(1, 4)
    def _(j):
        greet(r, (c + j) % 4)

    @pl.loop(0, 9)
    def _(j):
        greet((r + 16 * (1 + j // 3)) % 64, (c + 1 + j % 3) % 4)

    def pair_weights(low, high, cols):
        t_low, t_high = cols[:, 0:1], cols[:, 32:33]
        shared = jnp.maximum(jnp.minimum(high, t_high) - jnp.maximum(low, t_low), 0.0)
        return shared / (t_high - t_low)

    wxp[...] = pair_weights(
        src_rows[pl.ds(64 + chip, 1), :],
        src_rows[pl.ds(96 + chip, 1), :],
        pltpu.roll(tgt_cols[...], 64 - chip, 1),
    )
    wx = wxp[pl.ds(pl.multiple_of(TB * core, 8), TB), :]
    wx = pltpu.roll(wx, 64 * core, 1)
    wx64 = pltpu.roll(wx, 64, 1)
    wxp[0:TB, :] = wx64
    hi, lo = split(jnp.concatenate([wx, wx64], axis=0))
    wah[...] = hi
    wal[...] = lo
    third = wxp[pl.ds(pl.multiple_of(24 * half, 8), 24), :]
    hi, lo = split(jnp.concatenate([third, jnp.zeros((8, 128), F32)], axis=0))
    wbh[...] = hi
    wbl[...] = lo

    for zl in range(2):
        bx[zl, 8:56, :] = b_ref[zl]
    acc[...] = jnp.zeros_like(acc)

    def fold(a):
        out = a[:, 0:128]
        for i in range(1, 6):
            out = out + a[:, 128 * i : 128 * (i + 1)]
        return out

    def rows_of(a):
        return jnp.sum(a, axis=0, keepdims=True)

    lane8 = lanes((8, 768))
    row8 = lax.broadcasted_iota(jnp.int32, (8, 768), 0)
    square = jnp.zeros((8, 768), F32)
    rough = jnp.zeros((8, 768), F32)
    for g in range(6):
        a = [bx[zl, 8 + 8 * g : 16 + 8 * g, :] for zl in range(2)]
        d = a[0] - a[1]
        rough = rough + d * d
        for zl in range(2):
            square = square + a[zl] * a[zl]
            d = jnp.where(lane8 == 0, 0.0, a[zl] - pltpu.roll(a[zl], 1, 1))
            rough = rough + d * d
            if g > 0:
                d = a[zl] - bx[zl, 7 + 8 * g : 15 + 8 * g, :]
            else:
                d = jnp.where(row8 == 0, 0.0, a[zl] - pltpu.roll(a[zl], 1, 0))
            rough = rough + d * d
    tile_a[0, 0:1, :] = rows_of(fold(square))
    tile_a[0, 1:2, :] = rows_of(fold(rough))

    pl.semaphore_wait(barrier, 75)

    lane48 = lanes((TB, 128))

    def rim_copies(i):
        up, down = (r + 63) % 64, (r + 1) % 64
        left, right = (c + 3) % 4, (c + 1) % 4
        def copy(src, dst, d, peer):
            return pltpu.make_async_remote_copy(
                src_ref=src, dst_ref=dst, send_sem=hs_sem.at[i, d], recv_sem=hr_sem.at[i, d],
                device_id=peer, device_id_type=MESH,
            )
        return (
            copy(hs_row.at[i, 0], hr_row.at[i, 0], 0, (down, c)),
            copy(hs_row.at[i, 1], hr_row.at[i, 1], 1, (up, c)),
            copy(hs_col.at[i, 0], hr_col.at[i, 0], 2, (r, right)),
            copy(hs_col.at[i, 1], hr_col.at[i, 1], 3, (r, left)),
        )

    def rim_start(i, f):
        for zl in range(2):
            hs_row[i, 0, zl : zl + 1, :] = f[zl, 55:56, :]
            hs_row[i, 1, zl : zl + 1, :] = f[zl, 8:9, :]
        hs_col[i, 0] = jnp.where(
            lane48 == 127, f[0, 8:56, 640:768], pltpu.roll(f[1, 8:56, 640:768], 127, 1)
        )
        hs_col[i, 1] = jnp.where(lane48 == 0, f[0, 8:56, 0:128], pltpu.roll(f[1, 8:56, 0:128], 1, 1))
        for copy in rim_copies(i):
            copy.start()

    def rim_wait(i, f):
        for copy in rim_copies(i):
            copy.wait()
        for zl in range(2):
            f[zl, 7:8, :] = hr_row[i, 0, zl : zl + 1, :]
            f[zl, 56:57, :] = hr_row[i, 1, zl : zl + 1, :]

    rim_start(0, bx)

    spot_a = r % 16
    spot_b = y * 4 + c

    def sum_copy(i, stage, j):
        if stage == 0:
            peer = (16 * y + (spot_a + j) % 16, c)
            src, dst = tile_a.at[i], got_a.at[i, spot_a]
        else:
            other = (spot_b + j) % 16
            peer = (16 * (other // 4) + spot_a, other % 4)
            src, dst = tile_b.at[i], got_b.at[i, spot_b]
        return pltpu.make_async_remote_copy(
            src_ref=src, dst_ref=dst, send_sem=ts_sem.at[i, stage], recv_sem=tr_sem.at[i, stage],
            device_id=peer, device_id_type=MESH,
        )

    def sum_start(i, stage):
        @pl.loop(1, 16)
        def _(j):
            sum_copy(i, stage, j).start()

    def sum_wait(i, stage):
        got = got_a if stage == 0 else got_b
        tile = tile_a if stage == 0 else tile_b
        spot = spot_a if stage == 0 else spot_b
        got[i, pl.ds(spot, 1)] = tile[i][None]
        landed = got.at[i, 0:15]
        pltpu.make_async_copy(landed, landed, tr_sem.at[i, stage]).wait()
        total = got[i, 0]
        for j in range(1, 16):
            total = total + got[i, j]
        return total

    def compute(k):
        dy, dz = offsets(k)
        q = ((y + dy) % 4) * 8 + (z + dz) % 8
        wy = pair_weights(
            src_rows[pl.ds(q, 1), :], src_rows[pl.ds(32 + q, 1), :],
            pltpu.roll(tgt_cols[...], (128 - q) % 128, 1),
        )
        wyh, wyl = split(wy)
        fetch(k).wait()
        f = fbuf[k]
        for p in range(3):
            acc[p] = acc[p] + jnp.sum(f[p].reshape(8, 8, 128), axis=0)
        f = f.reshape(192, 128)
        fh, fo = split(f)
        nn = ((1,), (0,))
        g0 = product(wah[...], wal[...], fh[0:128], fo[0:128], nn)
        g1 = product(wbh[...], wbl[...], fh[64:192], fo[64:192], nn)
        gh, go = split(jnp.concatenate([g0, g1], axis=0))
        out = product(wyh, wyl, gh, go, ((1,), (1,)))
        sbuf[2 * k] = out[0:TB]
        sbuf[2 * k + 1] = out[TB : 2 * TB]

    def send(k):
        dy, dz = offsets(k)
        q = ((y + dy) % 4) * 8 + (z + dz) % 8
        for s in range(2):
            mine = jnp.logical_and(q == chip, core == s)

            @pl.when(mine)
            def _():
                pltpu.make_async_copy(
                    sbuf.at[2 * k + s], rb1.at[2 * k + core], rsem1.at[2 * k + core]
                ).start()

            @pl.when(jnp.logical_not(mine))
            def _():
                pltpu.make_async_remote_copy(
                    src_ref=sbuf.at[2 * k + s], dst_ref=rb1.at[2 * k + core],
                    send_sem=ssem, recv_sem=rsem1.at[2 * k + core],
                    device_id=(2 * q + s, c), device_id_type=MESH,
                ).start()

    def forward(k):
        dy, dz = offsets(k)
        to = (y - dy + 4) % 4
        zs = (z - dz + 8) % 8
        for s in range(2):
            got = rb1.at[2 * k + s]
            pltpu.make_async_copy(got, got, rsem1.at[2 * k + s]).wait()
            slot = c * 16 + zs * 2 + s

            @pl.when(to == c)
            def _():
                pltpu.make_async_copy(got, rb2.at[slot], rsem2.at[slot]).start()

            @pl.when(to != c)
            def _():
                pltpu.make_async_remote_copy(
                    src_ref=got, dst_ref=rb2.at[slot], send_sem=ssem2, recv_sem=rsem2.at[slot],
                    device_id=(r, to), device_id_type=MESH,
                ).start()

    def merge(k):
        dy, dz = offsets(k)
        zs = (z - dz + 8) % 8

        @pl.when((y - dy + 4) % 4 == c)
        def _():
            for cs in range(4):
                for s in range(2):
                    block = zs * 2 + s
                    slot = cs * 16 + block
                    got = rb2.at[slot]
                    pltpu.make_async_copy(got, got, rsem2.at[slot]).wait()
                    chunk = rb2[slot]
                    for p in range(3):
                        width = TB if p < 2 else 24
                        pos = TB * block + (24 * (cs % 2) if p == 2 else 0)
                        t0 = pos // 128
                        off = pos % 128
                        t1 = jnp.minimum(t0 + 1, 5)
                        turned = pltpu.roll(chunk, (off + 256 - TB * p) % 128, 1)
                        m = (cs // 2) * M + 3 * (cs % 2) + p
                        here = pl.ds(pl.multiple_of(t0 * 128, 128), 128)
                        inside = jnp.logical_and(lane48 >= off, lane48 < off + width)
                        R[m, :, here] = jnp.where(inside, turned, R[m, :, here])
                        there = pl.ds(pl.multiple_of(t1 * 128, 128), 128)
                        R[m, :, there] = jnp.where(lane48 < off + width - 128, turned, R[m, :, there])

    @pl.loop(0, NQ + LAG_MERGE)
    def _(it):
        @pl.when(it < NQ)
        def _():
            compute(it)

        @pl.when(jnp.logical_and(it >= 1, it <= NQ))
        def _():
            send(it - 1)

        @pl.when(it == NQ)
        def _():
            hf = half.astype(F32)
            for p in range(3):
                v = rows_of(acc[p])
                tile_a[0, 2 + p : 3 + p, :] = v * (1.0 - hf)
                tile_a[0, 5 + p : 6 + p, :] = v * hf
            sum_start(0, 0)

        @pl.when(it == NQ + 5)
        def _():
            tile_b[0] = sum_wait(0, 0)
            sum_start(0, 1)

        @pl.when(jnp.logical_and(it >= LAG_FORWARD, it < NQ + LAG_FORWARD))
        def _():
            forward(it - LAG_FORWARD)

        @pl.when(it >= LAG_MERGE)
        def _():
            merge(it - LAG_MERGE)

    for t in range(6):
        at = slice(128 * t, 128 * (t + 1))
        low = lax.rem(lanes((1, 128)) + 128 * t, TB) < 24
        for zl in range(2):
            m = [R[M * zl + i, :, at] for i in range(M)]
            rest = 1.0 - (m[0] + m[1] + m[3] + m[4])
            m[2], m[5] = jnp.where(low, m[2], rest - m[5]), jnp.where(low, rest - m[2], m[5])
            R[M * zl + 2, :, at] = m[2]
            R[M * zl + 5, :, at] = m[5]
            inverse = m[0] * param[0]
            heat = m[0] * param[M]
            for i in range(1, M):
                inverse = inverse + m[i] * param[i]
                heat = heat + m[i] * param[M + i]
            ix[zl, 8:56, at] = inverse
            cc[zl, :, at] = heat
    rim_start(1, ix)
    share_copy = pltpu.make_async_copy(R, shares_out, osem)
    share_copy.start()
    rim_wait(0, bx)

    early = jnp.sum(sum_wait(0, 1), axis=1, keepdims=True)
    norm = early[0:1]
    weight = early[2:3]
    mean_c = early[2:3] * param[M]
    mean_i = early[2:3] * param[0]
    for i in range(1, M):
        weight = weight + early[2 + i : 3 + i]
        mean_c = mean_c + early[2 + i : 3 + i] * param[M + i]
        mean_i = mean_i + early[2 + i : 3 + i] * param[i]
    sigma = mean_c / weight + early[1:2] / norm * weight / mean_i
    per = 1.0 / sigma

    def beside(i, f, zl, g):
        w = f[zl, 8 + 8 * g : 16 + 8 * g, :]
        above = f[zl, 7 + 8 * g : 15 + 8 * g, :]
        below = f[zl, 9 + 8 * g : 17 + 8 * g, :]
        lane = lanes((8, 128))
        hl = pltpu.roll(hr_col[i, 0, 8 * g : 8 * g + 8, :], 1 + zl, 1)
        hr = pltpu.roll(hr_col[i, 1, 8 * g : 8 * g + 8, :], 127 - zl, 1)
        left = pltpu.roll(w, 1, 1)
        right = pltpu.roll(w, 767, 1)
        left = jnp.concatenate([jnp.where(lane == 0, hl, left[:, 0:128]), left[:, 128:]], axis=1)
        right = jnp.concatenate(
            [right[:, 0:640], jnp.where(lane == 127, hr, right[:, 640:])], axis=1
        )
        return w, above, below, left, right

    def apply(i, f, out, out_row):
        odd = jnp.zeros((8, 768), F32)
        even = jnp.zeros((8, 768), F32)
        for zl in range(2):
            for g in range(6):
                at = slice(8 * g, 8 * g + 8)
                w, above, below, left, right = beside(i, f, zl, g)
                other = f[1 - zl, 8 + 8 * g : 16 + 8 * g, :]
                v = cc[zl, at, :] * w
                v = v + fz[at, :] * (w - other)
                v = v + fu[zl, at, :] * (w - above) + fd[zl, at, :] * (w - below)
                v = v + fl[zl, at, :] * (w - left) + fr[zl, at, :] * (w - right)
                out[zl, out_row + 8 * g : out_row + 8 * g + 8, :] = v
                odd = odd + w * v
                even = even + v * v
        return rows_of(fold(odd)), rows_of(fold(even))

    rim_wait(1, ix)
    zero, one = jnp.float32(0.0), jnp.float32(1.0)
    top = jnp.where(r == 0, zero, one)
    bottom = jnp.where(r == 63, zero, one)
    first = jnp.where(c == 0, zero, one)
    last = jnp.where(c == 3, zero, one)
    twice = jnp.broadcast_to(2.0 * per, (8, 768))
    for zl in range(2):
        for g in range(6):
            at = slice(8 * g, 8 * g + 8)
            w, above, below, left, right = beside(1, ix, zl, g)
            f = twice / (w + above)
            fu[zl, at, :] = f * jnp.where(row8 == 0, top, one) if g == 0 else f
            f = twice / (w + below)
            fd[zl, at, :] = f * jnp.where(row8 == 7, bottom, one) if g == 5 else f
            fl[zl, at, :] = twice / (w + left) * jnp.where(lane8 == 0, first, one)
            fr[zl, at, :] = twice / (w + right) * jnp.where(lane8 == 767, last, one)
            if zl == 0:
                fz[at, :] = twice / (w + ix[1, 8 + 8 * g : 16 + 8 * g, :])
            cc[zl, at, :] = cc[zl, at, :] * per - 1.0

    tile_a[1] = jnp.zeros((8, 128), F32)
    s1, s2 = apply(0, bx, v1, 8)
    rim_start(2, v1)
    tile_a[1, 0:1, :] = s1
    tile_a[1, 1:2, :] = s2
    rim_wait(2, v1)
    s1, s2 = apply(2, v1, v2, 8)
    rim_start(3, v2)
    tile_a[1, 2:3, :] = s1
    tile_a[1, 3:4, :] = s2
    rim_wait(3, v2)
    s1, s2 = apply(3, v2, v3, 0)
    tile_a[1, 4:5, :] = s1
    sum_start(1, 0)
    tile_b[1] = sum_wait(1, 0)
    sum_start(1, 1)
    sums = jnp.sum(sum_wait(1, 1), axis=1, keepdims=True)
    mom = [norm] + [sums[i : i + 1] for i in range(5)]

    def inner(p, q):
        total = None
        for i, pi in enumerate(p):
            for j, qj in enumerate(q):
                term = pi * qj * mom[i + j]
                total = term if total is None else total + term
        return total

    def combine(p, q, s):
        size = max(len(p), len(q))
        out = []
        for i in range(size):
            if i < len(p) and i < len(q):
                out.append(p[i] + s * q[i])
            else:
                out.append(p[i] if i < len(p) else s * q[i])
        return out

    unit = jnp.ones((1, 1), F32)
    x, res, direction, rr = [], [unit], [unit], norm
    for it in range(3):
        n = len(direction)
        applied = [direction[0] * sigma]
        applied += [(direction[i] + direction[i - 1]) * sigma for i in range(1, n)]
        applied += [direction[n - 1] * sigma]
        alpha = rr / inner(direction, applied)
        x = combine(x, direction, alpha)
        res = combine(res, applied, -alpha)
        if it < 2:
            new = inner(res, res)
            direction = combine(res, direction, new / rr)
            rr = new

    for zl in range(2):
        for g in range(6):
            at = slice(8 * g, 8 * g + 8)
            ext = slice(8 + 8 * g, 16 + 8 * g)
            base = (bx[zl, ext, :], v1[zl, ext, :], v2[zl, ext, :], v3[zl, at, :])
            out = x[0] * base[0]
            for i in range(1, 3):
                out = out + x[i] * base[i]
            x_out[zl, at, :] = out
            out = res[0] * base[0]
            for i in range(1, 4):
                out = out + res[i] * base[i]
            r_out[zl, at, :] = out

    share_copy.wait()
    sent = sbuf.at[0:63]
    pltpu.make_async_copy(sent, sent, ssem).wait()
    sent = rb1.at[0:48]
    pltpu.make_async_copy(sent, sent, ssem2).wait()
    for i in range(2):
        for stage in range(2):
            sent = got_a.at[i, 0:15]
            pltpu.make_async_copy(sent, sent, ts_sem.at[i, stage]).wait()


def per_device(
    fractions_source,
    x_source_edges,
    x_target_edges,
    y_source_edges,
    y_target_edges,
    conductivity_table,
    capacity,
    thermal_source_term,
):
    def sides(edges, width):
        edges = edges.astype(F32)
        return [edges[:-1].reshape(NQ, width), edges[1:].reshape(NQ, width)]

    src_rows = jnp.concatenate(sides(y_source_edges, 128) + sides(x_source_edges, 128), axis=0)
    tgt_cols = jnp.concatenate(sides(y_target_edges, 96) + sides(x_target_edges, 96), axis=0).T
    param = jnp.concatenate([16.0 / conductivity_table.astype(F32), capacity])
    field = jax.ShapeDtypeStruct((2, TB, 768), F32)
    vmem = pl.BlockSpec(memory_space=pltpu.VMEM)
    anywhere = pl.BlockSpec(memory_space=pl.ANY)
    ext = VM((2, 64, 768), F32)
    inner = VM((2, TB, 768), F32)
    return pl.pallas_call(
        kernel,
        out_shape=(jax.ShapeDtypeStruct((2 * M, TB, 768), F32), field, field),
        in_specs=[anywhere, vmem, vmem, pl.BlockSpec(memory_space=pltpu.SMEM), vmem],
        out_specs=(anywhere, vmem, vmem),
        scratch_shapes=[
            VM((NQ, 3, 64, 128), F32),
            VM((96, 128), F32),
            VM((96, 128), BF16), VM((96, 128), BF16),
            VM((32, 128), BF16), VM((32, 128), BF16),
            VM((64, TB, 128), F32), VM((64, TB, 128), F32), VM((64, TB, 128), F32),
            VM((2 * M, TB, 768), F32),
            ext, ext, ext, ext, inner, inner,
            inner, inner, inner, inner, VM((TB, 768), F32),
            VM((4, 2, 2, 768), F32), VM((4, 2, 2, 768), F32),
            VM((4, 2, TB, 128), F32), VM((4, 2, TB, 128), F32),
            VM((3, 8, 128), F32),
            VM((2, 8, 128), F32), VM((2, 16, 8, 128), F32),
            VM((2, 8, 128), F32), VM((2, 16, 8, 128), F32),
            DMA((NQ,)), DMA, DMA((64,)), DMA, DMA((64,)),
            DMA((4, 4)), DMA((4, 4)), DMA((2, 2)), DMA((2, 2)), DMA,
        ],
        compiler_params=pltpu.CompilerParams(
            collective_id=0, has_side_effects=True, vmem_limit_bytes=48 * 2**20
        ),
    )(fractions_source, src_rows, tgt_cols, param, thermal_source_term)


def solution(mesh):
    placed = (P("col", "row", None), P(), P(), P(), P(), P(), P(), P(None, "row", "col"))
    return jax.shard_map(
        per_device,
        mesh=mesh,
        in_specs=placed,
        out_specs=(P(None, "row", "col"), P(None, "row", "col"), P(None, "row", "col")),
        check_vma=False,
    )
```

```python
import jax
import jax.numpy as jnp
from jax import lax
from jax.experimental import pallas as pl
from jax.experimental.pallas import tpu as pltpu
from jax.sharding import PartitionSpec as P

M = 6
TB = 48
NQ = 32
AHEAD = 14
LAG_FORWARD = 8
LAG_MERGE = 14
MESH = pl.DeviceIdType.MESH
F32 = jnp.float32
BF16 = jnp.bfloat16
VM = pltpu.VMEM
DMA = pltpu.SemaphoreType.DMA


def split(a):
    high = a.astype(BF16)
    return high, (a - high.astype(F32)).astype(BF16)


def product(ah, al, bh, bl, dims):
    def dot(p, q):
        return lax.dot_general(p, q, (dims, ((), ())), preferred_element_type=F32)

    return dot(ah, bh) + (dot(ah, bl) + dot(al, bh))


def offsets(k):
    g, s = k // 8, k % 2
    dz = jnp.where(s == 0, 4 - g, jnp.where(g == 0, 0, 4 + g))
    return (k // 2) % 4, dz


def lanes(shape):
    return lax.broadcasted_iota(jnp.int32, shape, len(shape) - 1)


def kernel(
    frac, xs_edges, xt_edges, ys_edges, yt_edges, table_in, capacity_in, b_ref, R, x_out, r_out,
    xs_line, xt_line, ys_line, yt_line, xs_rows, xt_rows, ys_rows, yt_rows,
    table, capacity, fbuf, wxp, wah, wal, wbh, wbl, sbuf, rb1, rb2, bx, ix, v1, v2, v3, cc,
    fu, fd, fl, fr, fz, hs_row, hr_row, hs_col, hr_col, acc, tile_a, got_a, tile_b, got_b,
    esem, fsem, ssem, rsem1, ssem2, rsem2, hs_sem, hr_sem, ts_sem, tr_sem,
):
    r = lax.axis_index("row")
    c = lax.axis_index("col")
    core = r % 2
    chip = r // 2
    y, z = chip // 8, chip % 8
    half = c % 2

    lines = ((xs_edges, xs_line), (xt_edges, xt_line), (ys_edges, ys_line), (yt_edges, yt_line))
    early_copies = [pltpu.make_async_copy(a, b, esem.at[i]) for i, (a, b) in enumerate(lines)]
    early_copies.append(pltpu.make_async_copy(b_ref, bx.at[:, 8:56, :], esem.at[4]))
    early_copies.append(pltpu.make_async_copy(table_in, table, esem.at[5]))
    early_copies.append(pltpu.make_async_copy(capacity_in, capacity, esem.at[6]))
    for copy in early_copies:
        copy.start()

    def fetch(k):
        dy, dz = offsets(k)
        q = ((y + dy) % 4) * 8 + (z + dz) % 8
        return pltpu.make_async_copy(
            frac.at[:, :, pl.ds(pl.multiple_of(q * 128, 128), 128)], fbuf.at[k], fsem.at[k]
        )

    @pl.loop(0, NQ)
    def _(k):
        fetch(k).start()

    barrier = pltpu.get_barrier_semaphore()

    def greet(row, col):
        pl.semaphore_signal(barrier, inc=1, device_id=(row, col), device_id_type=MESH)

    @pl.loop(1, 64)
    def _(j):
        greet((r + j) % 64, c)

    @pl.loop(1, 4)
    def _(j):
        greet(r, (c + j) % 4)

    @pl.loop(0, 9)
    def _(j):
        greet((r + 16 * (1 + j // 3)) % 64, (c + 1 + j % 3) % 4)

    for i, (line, rows) in enumerate(
        ((xs_line, xs_rows), (xt_line, xt_rows), (ys_line, ys_rows), (yt_line, yt_rows))
    ):
        early_copies[i].wait()
        for q in range(line.shape[0] // 128):
            part = line[128 * q : 128 * (q + 1)]
            rows[q : q + 1, :] = part.astype(F32).reshape(1, 128)
        q = line.shape[0] // 128
        rows[q : q + 1, 0:1] = line[128 * q : 128 * q + 1].astype(F32).reshape(1, 1)

    lane1 = lanes((1, 128))

    def pair_weights(src, tgt, q):
        low = src[pl.ds(q, 1), :]
        high = pltpu.roll(jnp.where(lane1 == 0, src[pl.ds(q + 1, 1), :], low), 127, 1)
        row = 96 * q // 128
        off = 96 * q % 128
        line = jnp.where(lane1 >= off, tgt[pl.ds(row, 1), :], tgt[pl.ds(row + 1, 1), :])
        line = pltpu.roll(line, (128 - off) % 128, 1)
        cols = jnp.broadcast_to(line, (128, 128)).T
        t_low, t_high = cols[0:96], cols[1:97]
        shared = jnp.maximum(jnp.minimum(high, t_high) - jnp.maximum(low, t_low), 0.0)
        return shared / (t_high - t_low)

    wxp[...] = pair_weights(xs_rows, xt_rows, chip)
    wx = wxp[pl.ds(pl.multiple_of(TB * core, 8), TB), :]
    wx = pltpu.roll(wx, 64 * core, 1)
    wx64 = pltpu.roll(wx, 64, 1)
    wxp[0:TB, :] = wx64
    hi, lo = split(jnp.concatenate([wx, wx64], axis=0))
    wah[...] = hi
    wal[...] = lo
    third = wxp[pl.ds(pl.multiple_of(24 * half, 8), 24), :]
    hi, lo = split(jnp.concatenate([third, jnp.zeros((8, 128), F32)], axis=0))
    wbh[...] = hi
    wbl[...] = lo

    for copy in early_copies[4:]:
        copy.wait()
    acc[...] = jnp.zeros_like(acc)

    def fold(a):
        out = a[:, 0:128]
        for i in range(1, 6):
            out = out + a[:, 128 * i : 128 * (i + 1)]
        return out

    def rows_of(a):
        return jnp.sum(a, axis=0, keepdims=True)

    lane8 = lanes((8, 768))
    row8 = lax.broadcasted_iota(jnp.int32, (8, 768), 0)
    square = jnp.zeros((8, 768), F32)
    rough = jnp.zeros((8, 768), F32)
    for g in range(6):
        a = [bx[zl, 8 + 8 * g : 16 + 8 * g, :] for zl in range(2)]
        d = a[0] - a[1]
        rough = rough + d * d
        for zl in range(2):
            square = square + a[zl] * a[zl]
            d = jnp.where(lane8 == 0, 0.0, a[zl] - pltpu.roll(a[zl], 1, 1))
            rough = rough + d * d
            if g > 0:
                d = a[zl] - bx[zl, 7 + 8 * g : 15 + 8 * g, :]
            else:
                d = jnp.where(row8 == 0, 0.0, a[zl] - pltpu.roll(a[zl], 1, 0))
            rough = rough + d * d
    tile_a[0, 0:1, :] = rows_of(fold(square))
    tile_a[0, 1:2, :] = rows_of(fold(rough))

    lane48 = lanes((TB, 128))

    def rim_copies(i):
        up, down = (r + 63) % 64, (r + 1) % 64
        left, right = (c + 3) % 4, (c + 1) % 4
        def copy(src, dst, d, peer):
            return pltpu.make_async_remote_copy(
                src_ref=src, dst_ref=dst, send_sem=hs_sem.at[i, d], recv_sem=hr_sem.at[i, d],
                device_id=peer, device_id_type=MESH,
            )
        return (
            copy(hs_row.at[i, 0], hr_row.at[i, 0], 0, (down, c)),
            copy(hs_row.at[i, 1], hr_row.at[i, 1], 1, (up, c)),
            copy(hs_col.at[i, 0], hr_col.at[i, 0], 2, (r, right)),
            copy(hs_col.at[i, 1], hr_col.at[i, 1], 3, (r, left)),
        )

    def rim_start(i, f):
        for zl in range(2):
            hs_row[i, 0, zl : zl + 1, :] = f[zl, 55:56, :]
            hs_row[i, 1, zl : zl + 1, :] = f[zl, 8:9, :]
        hs_col[i, 0] = jnp.where(
            lane48 == 127, f[0, 8:56, 640:768], pltpu.roll(f[1, 8:56, 640:768], 127, 1)
        )
        hs_col[i, 1] = jnp.where(lane48 == 0, f[0, 8:56, 0:128], pltpu.roll(f[1, 8:56, 0:128], 1, 1))
        for copy in rim_copies(i):
            copy.start()

    def rim_wait(i, f):
        for copy in rim_copies(i):
            copy.wait()
        for zl in range(2):
            f[zl, 7:8, :] = hr_row[i, 0, zl : zl + 1, :]
            f[zl, 56:57, :] = hr_row[i, 1, zl : zl + 1, :]

    spot_a = r % 16
    spot_b = y * 4 + c

    def sum_copy(i, stage, j):
        if stage == 0:
            peer = (16 * y + (spot_a + j) % 16, c)
            src, dst = tile_a.at[i], got_a.at[i, spot_a]
        else:
            other = (spot_b + j) % 16
            peer = (16 * (other // 4) + spot_a, other % 4)
            src, dst = tile_b.at[i], got_b.at[i, spot_b]
        return pltpu.make_async_remote_copy(
            src_ref=src, dst_ref=dst, send_sem=ts_sem.at[i, stage], recv_sem=tr_sem.at[i, stage],
            device_id=peer, device_id_type=MESH,
        )

    def sum_start(i, stage):
        @pl.loop(1, 16)
        def _(j):
            sum_copy(i, stage, j).start()

    def sum_wait(i, stage):
        got = got_a if stage == 0 else got_b
        tile = tile_a if stage == 0 else tile_b
        spot = spot_a if stage == 0 else spot_b
        got[i, pl.ds(spot, 1)] = tile[i][None]
        landed = got.at[i, 0:15]
        pltpu.make_async_copy(landed, landed, tr_sem.at[i, stage]).wait()
        total = got[i, 0]
        for j in range(1, 16):
            total = total + got[i, j]
        return total

    def compute(k):
        dy, dz = offsets(k)
        q = ((y + dy) % 4) * 8 + (z + dz) % 8
        wy = pair_weights(ys_rows, yt_rows, q)
        wyh, wyl = split(wy)
        fetch(k).wait()
        f = fbuf[k]
        for p in range(3):
            acc[p] = acc[p] + jnp.sum(f[p].reshape(8, 8, 128), axis=0)
        f = f.reshape(192, 128)
        fh, fo = split(f)
        nn = ((1,), (0,))
        g0 = product(wah[...], wal[...], fh[0:128], fo[0:128], nn)
        g1 = product(wbh[...], wbl[...], fh[64:192], fo[64:192], nn)
        gh, go = split(jnp.concatenate([g0, g1], axis=0))
        out = product(wyh, wyl, gh, go, ((1,), (1,)))
        sbuf[2 * k] = out[0:TB]
        sbuf[2 * k + 1] = out[TB : 2 * TB]

    def send(k):
        dy, dz = offsets(k)
        q = ((y + dy) % 4) * 8 + (z + dz) % 8
        for s in range(2):
            mine = jnp.logical_and(q == chip, core == s)

            @pl.when(mine)
            def _():
                pltpu.make_async_copy(
                    sbuf.at[2 * k + s], rb1.at[2 * k + core], rsem1.at[2 * k + core]
                ).start()

            @pl.when(jnp.logical_not(mine))
            def _():
                pltpu.make_async_remote_copy(
                    src_ref=sbuf.at[2 * k + s], dst_ref=rb1.at[2 * k + core],
                    send_sem=ssem, recv_sem=rsem1.at[2 * k + core],
                    device_id=(2 * q + s, c), device_id_type=MESH,
                ).start()

    def forward(k):
        dy, dz = offsets(k)
        to = (y - dy + 4) % 4
        zs = (z - dz + 8) % 8
        for s in range(2):
            got = rb1.at[2 * k + s]
            pltpu.make_async_copy(got, got, rsem1.at[2 * k + s]).wait()
            slot = c * 16 + zs * 2 + s

            @pl.when(to == c)
            def _():
                pltpu.make_async_copy(got, rb2.at[slot], rsem2.at[slot]).start()

            @pl.when(to != c)
            def _():
                pltpu.make_async_remote_copy(
                    src_ref=got, dst_ref=rb2.at[slot], send_sem=ssem2, recv_sem=rsem2.at[slot],
                    device_id=(r, to), device_id_type=MESH,
                ).start()

    def merge(k):
        dy, dz = offsets(k)
        zs = (z - dz + 8) % 8

        @pl.when((y - dy + 4) % 4 == c)
        def _():
            for cs in range(4):
                for s in range(2):
                    block = zs * 2 + s
                    slot = cs * 16 + block
                    got = rb2.at[slot]
                    pltpu.make_async_copy(got, got, rsem2.at[slot]).wait()
                    chunk = rb2[slot]
                    for p in range(3):
                        width = TB if p < 2 else 24
                        pos = TB * block + (24 * (cs % 2) if p == 2 else 0)
                        t0 = pos // 128
                        off = pos % 128
                        t1 = jnp.minimum(t0 + 1, 5)
                        turned = pltpu.roll(chunk, (off + 256 - TB * p) % 128, 1)
                        m = (cs // 2) * M + 3 * (cs % 2) + p
                        here = pl.ds(pl.multiple_of(t0 * 128, 128), 128)
                        inside = jnp.logical_and(lane48 >= off, lane48 < off + width)
                        R[m, :, here] = jnp.where(inside, turned, R[m, :, here])
                        there = pl.ds(pl.multiple_of(t1 * 128, 128), 128)
                        R[m, :, there] = jnp.where(lane48 < off + width - 128, turned, R[m, :, there])

    @pl.loop(0, AHEAD)
    def _(k):
        compute(k)

    pl.semaphore_wait(barrier, 75)

    @pl.loop(0, AHEAD)
    def _(k):
        send(k)

    rim_start(0, bx)

    @pl.loop(0, NQ + LAG_MERGE)
    def _(it):
        @pl.when(it < NQ - AHEAD)
        def _():
            compute(it + AHEAD)

        @pl.when(jnp.logical_and(it >= 1, it <= NQ - AHEAD))
        def _():
            send(it + AHEAD - 1)

        @pl.when(it == NQ - AHEAD)
        def _():
            hf = half.astype(F32)
            for p in range(3):
                v = rows_of(acc[p])
                tile_a[0, 2 + p : 3 + p, :] = v * (1.0 - hf)
                tile_a[0, 5 + p : 6 + p, :] = v * hf
            sum_start(0, 0)

        @pl.when(it == NQ - AHEAD + 6)
        def _():
            tile_b[0] = sum_wait(0, 0)
            sum_start(0, 1)

        @pl.when(jnp.logical_and(it >= LAG_FORWARD, it < NQ + LAG_FORWARD))
        def _():
            forward(it - LAG_FORWARD)

        @pl.when(it >= LAG_MERGE)
        def _():
            merge(it - LAG_MERGE)

    param = [16.0 / jnp.full((1, 128), table[i].astype(F32)) for i in range(M)]
    param += [jnp.full((1, 128), capacity[i]) for i in range(M)]

    for t in range(6):
        at = slice(128 * t, 128 * (t + 1))
        low = lax.rem(lanes((1, 128)) + 128 * t, TB) < 24
        for zl in range(2):
            m = [R[M * zl + i, :, at] for i in range(M)]
            rest = 1.0 - (m[0] + m[1] + m[3] + m[4])
            m[2], m[5] = jnp.where(low, m[2], rest - m[5]), jnp.where(low, rest - m[2], m[5])
            R[M * zl + 2, :, at] = m[2]
            R[M * zl + 5, :, at] = m[5]
            inverse = m[0] * param[0]
            heat = m[0] * param[M]
            for i in range(1, M):
                inverse = inverse + m[i] * param[i]
                heat = heat + m[i] * param[M + i]
            ix[zl, 8:56, at] = inverse
            cc[zl, :, at] = heat
    rim_start(1, ix)
    rim_wait(0, bx)

    param = [a[:, 0:1] for a in param]
    early = jnp.sum(sum_wait(0, 1), axis=1, keepdims=True)
    norm = early[0:1]
    weight = early[2:3]
    mean_c = early[2:3] * param[M]
    mean_i = early[2:3] * param[0]
    for i in range(1, M):
        weight = weight + early[2 + i : 3 + i]
        mean_c = mean_c + early[2 + i : 3 + i] * param[M + i]
        mean_i = mean_i + early[2 + i : 3 + i] * param[i]
    sigma = mean_c / weight + early[1:2] / norm * weight / mean_i
    per = 1.0 / sigma

    def beside(i, f, zl, g):
        w = f[zl, 8 + 8 * g : 16 + 8 * g, :]
        above = f[zl, 7 + 8 * g : 15 + 8 * g, :]
        below = f[zl, 9 + 8 * g : 17 + 8 * g, :]
        lane = lanes((8, 128))
        hl = pltpu.roll(hr_col[i, 0, 8 * g : 8 * g + 8, :], 1 + zl, 1)
        hr = pltpu.roll(hr_col[i, 1, 8 * g : 8 * g + 8, :], 127 - zl, 1)
        left = pltpu.roll(w, 1, 1)
        right = pltpu.roll(w, 767, 1)
        left = jnp.concatenate([jnp.where(lane == 0, hl, left[:, 0:128]), left[:, 128:]], axis=1)
        right = jnp.concatenate(
            [right[:, 0:640], jnp.where(lane == 127, hr, right[:, 640:])], axis=1
        )
        return w, above, below, left, right

    def apply(i, f, out, out_row):
        odd = jnp.zeros((8, 768), F32)
        even = jnp.zeros((8, 768), F32)
        for zl in range(2):
            for g in range(6):
                at = slice(8 * g, 8 * g + 8)
                w, above, below, left, right = beside(i, f, zl, g)
                other = f[1 - zl, 8 + 8 * g : 16 + 8 * g, :]
                v = cc[zl, at, :] * w
                v = v + fz[at, :] * (w - other)
                v = v + fu[zl, at, :] * (w - above) + fd[zl, at, :] * (w - below)
                v = v + fl[zl, at, :] * (w - left) + fr[zl, at, :] * (w - right)
                out[zl, out_row + 8 * g : out_row + 8 * g + 8, :] = v
                odd = odd + w * v
                even = even + v * v
        return rows_of(fold(odd)), rows_of(fold(even))

    rim_wait(1, ix)
    zero, one = jnp.float32(0.0), jnp.float32(1.0)
    top = jnp.where(r == 0, zero, one)
    bottom = jnp.where(r == 63, zero, one)
    first = jnp.where(c == 0, zero, one)
    last = jnp.where(c == 3, zero, one)
    twice = jnp.broadcast_to(2.0 * per, (8, 768))
    for zl in range(2):
        for g in range(6):
            at = slice(8 * g, 8 * g + 8)
            w, above, below, left, right = beside(1, ix, zl, g)
            f = twice / (w + above)
            fu[zl, at, :] = f * jnp.where(row8 == 0, top, one) if g == 0 else f
            f = twice / (w + below)
            fd[zl, at, :] = f * jnp.where(row8 == 7, bottom, one) if g == 5 else f
            fl[zl, at, :] = twice / (w + left) * jnp.where(lane8 == 0, first, one)
            fr[zl, at, :] = twice / (w + right) * jnp.where(lane8 == 767, last, one)
            if zl == 0:
                fz[at, :] = twice / (w + ix[1, 8 + 8 * g : 16 + 8 * g, :])
            cc[zl, at, :] = cc[zl, at, :] * per - 1.0

    tile_a[1] = jnp.zeros((8, 128), F32)
    s1, s2 = apply(0, bx, v1, 8)
    rim_start(2, v1)
    tile_a[1, 0:1, :] = s1
    tile_a[1, 1:2, :] = s2
    rim_wait(2, v1)
    s1, s2 = apply(2, v1, v2, 8)
    rim_start(3, v2)
    tile_a[1, 2:3, :] = s1
    tile_a[1, 3:4, :] = s2
    rim_wait(3, v2)
    s1, s2 = apply(3, v2, v3, 0)
    tile_a[1, 4:5, :] = s1
    sum_start(1, 0)
    tile_b[1] = sum_wait(1, 0)
    sum_start(1, 1)
    sums = jnp.sum(sum_wait(1, 1), axis=1, keepdims=True)
    mom = [norm] + [sums[i : i + 1] for i in range(5)]

    def inner(p, q):
        total = None
        for i, pi in enumerate(p):
            for j, qj in enumerate(q):
                term = pi * qj * mom[i + j]
                total = term if total is None else total + term
        return total

    def combine(p, q, s):
        size = max(len(p), len(q))
        out = []
        for i in range(size):
            if i < len(p) and i < len(q):
                out.append(p[i] + s * q[i])
            else:
                out.append(p[i] if i < len(p) else s * q[i])
        return out

    unit = jnp.ones((1, 1), F32)
    x, res, direction, rr = [], [unit], [unit], norm
    for it in range(3):
        n = len(direction)
        applied = [direction[0] * sigma]
        applied += [(direction[i] + direction[i - 1]) * sigma for i in range(1, n)]
        applied += [direction[n - 1] * sigma]
        alpha = rr / inner(direction, applied)
        x = combine(x, direction, alpha)
        res = combine(res, applied, -alpha)
        if it < 2:
            new = inner(res, res)
            direction = combine(res, direction, new / rr)
            rr = new

    for zl in range(2):
        for g in range(6):
            at = slice(8 * g, 8 * g + 8)
            ext = slice(8 + 8 * g, 16 + 8 * g)
            base = (bx[zl, ext, :], v1[zl, ext, :], v2[zl, ext, :], v3[zl, at, :])
            out = x[0] * base[0]
            for i in range(1, 3):
                out = out + x[i] * base[i]
            x_out[zl, at, :] = out
            out = res[0] * base[0]
            for i in range(1, 4):
                out = out + res[i] * base[i]
            r_out[zl, at, :] = out

    sent = sbuf.at[0:63]
    pltpu.make_async_copy(sent, sent, ssem).wait()
    sent = rb1.at[0:48]
    pltpu.make_async_copy(sent, sent, ssem2).wait()
    for i in range(2):
        for stage in range(2):
            sent = got_a.at[i, 0:15]
            pltpu.make_async_copy(sent, sent, ts_sem.at[i, stage]).wait()


def put_out(*refs):
    sem = refs[6]
    copies = [pltpu.make_async_copy(refs[i], refs[3 + i], sem.at[i]) for i in range(3)]
    for copy in copies:
        copy.start()
    for copy in copies:
        copy.wait()


def per_device(
    fractions_source,
    x_source_edges,
    x_target_edges,
    y_source_edges,
    y_target_edges,
    conductivity_table,
    capacity,
    thermal_source_term,
):
    field = jax.ShapeDtypeStruct((2, TB, 768), F32)
    vmem = pl.BlockSpec(memory_space=pltpu.VMEM)
    hbm = pl.BlockSpec(memory_space=pltpu.HBM)
    shapes = (jax.ShapeDtypeStruct((2 * M, TB, 768), F32), field, field)
    ext = VM((2, 64, 768), F32)
    inner = VM((2, TB, 768), F32)
    made = pl.pallas_call(
        kernel,
        out_shape=shapes,
        in_specs=[hbm] * 8,
        out_specs=(vmem, vmem, vmem),
        scratch_shapes=[
            VM((4097,), jnp.int32), VM((3073,), jnp.int32),
            VM((4097,), jnp.int32), VM((3073,), jnp.int32),
            VM((40, 128), F32), VM((32, 128), F32), VM((40, 128), F32), VM((32, 128), F32),
            pltpu.SMEM((M,), jnp.int32), pltpu.SMEM((M,), F32),
            VM((NQ, 3, 64, 128), F32),
            VM((96, 128), F32),
            VM((96, 128), BF16), VM((96, 128), BF16),
            VM((32, 128), BF16), VM((32, 128), BF16),
            VM((64, TB, 128), F32), VM((64, TB, 128), F32), VM((64, TB, 128), F32),
            ext, ext, ext, ext, inner, inner,
            inner, inner, inner, inner, VM((TB, 768), F32),
            VM((4, 2, 2, 768), F32), VM((4, 2, 2, 768), F32),
            VM((4, 2, TB, 128), F32), VM((4, 2, TB, 128), F32),
            VM((3, 8, 128), F32),
            VM((2, 8, 128), F32), VM((2, 16, 8, 128), F32),
            VM((2, 8, 128), F32), VM((2, 16, 8, 128), F32),
            DMA((7,)), DMA((NQ,)), DMA, DMA((64,)), DMA, DMA((64,)),
            DMA((4, 4)), DMA((4, 4)), DMA((2, 2)), DMA((2, 2)),
        ],
        compiler_params=pltpu.CompilerParams(
            collective_id=0, has_side_effects=True, vmem_limit_bytes=48 * 2**20
        ),
    )(
        *[
            pltpu.with_memory_space_constraint(a, pltpu.HBM)
            for a in (
                fractions_source, x_source_edges, x_target_edges, y_source_edges, y_target_edges,
                conductivity_table, capacity, thermal_source_term,
            )
        ]
    )
    return pl.pallas_call(
        put_out,
        out_shape=shapes,
        in_specs=[pl.BlockSpec(memory_space=pl.ANY)] * 3,
        out_specs=(hbm, hbm, hbm),
        scratch_shapes=[DMA((3,))],
        compiler_params=pltpu.CompilerParams(vmem_limit_bytes=2**20),
    )(*made)


def solution(mesh):
    placed = (P("col", "row", None), P(), P(), P(), P(), P(), P(), P(None, "row", "col"))
    return jax.shard_map(
        per_device,
        mesh=mesh,
        in_specs=placed,
        out_specs=(P(None, "row", "col"), P(None, "row", "col"), P(None, "row", "col")),
        check_vma=False,
    )
```

```python
import jax
import jax.numpy as jnp
from jax import lax
from jax.experimental import pallas as pl
from jax.experimental.pallas import tpu as pltpu
from jax.sharding import PartitionSpec as P

M = 6
TB = 48
NQ = 32
GROUP = 4
WINDOW = 20
LAG_MERGE = 16
MESH = pl.DeviceIdType.MESH
F32 = jnp.float32
BF16 = jnp.bfloat16
VM = pltpu.VMEM
DMA = pltpu.SemaphoreType.DMA


def split(a):
    high = a.astype(BF16)
    return high, (a - high.astype(F32)).astype(BF16)


def dot(a, b, dims):
    return lax.dot_general(a, b, (dims, ((), ())), preferred_element_type=F32)


def offsets(k, c):
    g, s = k // 8, k % 2
    dz = jnp.where(s == 0, 4 - g, jnp.where(g == 0, 0, 4 + g))
    return (k // 2 + c) % 4, dz


def lanes(shape):
    return lax.broadcasted_iota(jnp.int32, shape, len(shape) - 1)


def kernel(
    frac, xs_edges, xt_edges, ys_edges, yt_edges, table_in, capacity_in, b_ref, R, x_out, r_out,
    xs_line, xt_line, ys_line, yt_line, xs_rows, xt_rows, ys_rows, yt_rows,
    table, capacity, fbuf, wxp, wx_all, sbuf, rb1, rb2, bx, ix, v1, v2, v3, cc,
    fu, fd, fl, fr, fz, hs_row, hr_row, hs_col, hr_col, acc, tile_a, got_a, tile_b, got_b,
    esem, fsem, ssem, rsem1, ssem2, rsem2, hs_sem, hr_sem, ts_sem, tr_sem,
):
    r = lax.axis_index("row")
    c = lax.axis_index("col")
    core = r % 2
    chip = r // 2
    y, z = chip // 8, chip % 8
    half = c % 2

    lines = ((xs_edges, xs_line), (xt_edges, xt_line), (ys_edges, ys_line), (yt_edges, yt_line))
    early_copies = [pltpu.make_async_copy(a, b, esem.at[i]) for i, (a, b) in enumerate(lines)]
    early_copies.append(pltpu.make_async_copy(b_ref, bx.at[:, 8:56, :], esem.at[4]))
    early_copies.append(pltpu.make_async_copy(table_in, table, esem.at[5]))
    early_copies.append(pltpu.make_async_copy(capacity_in, capacity, esem.at[6]))
    for copy in early_copies:
        copy.start()

    def fetch(k):
        dy, dz = offsets(k, c)
        q = ((y + dy) % 4) * 8 + (z + dz) % 8
        return pltpu.make_async_copy(
            frac.at[:, :, pl.ds(pl.multiple_of(q * 128, 128), 128)], fbuf.at[k], fsem.at[k]
        )

    @pl.loop(0, NQ)
    def _(k):
        fetch(k).start()

    barrier = pltpu.get_barrier_semaphore()

    def greet(row, col):
        pl.semaphore_signal(barrier, inc=1, device_id=(row, col), device_id_type=MESH)

    @pl.loop(1, 64)
    def _(j):
        greet(16 * y + (r + j // 4) % 16, (c + j % 4) % 4)

    @pl.loop(1, 4)
    def _(j):
        greet((r + 16 * j) % 64, c)

    greet((r + 1) % 64, c)
    greet((r + 63) % 64, c)

    @pl.loop(0, 9)
    def _(j):
        greet((r + 16 * (1 + j // 3)) % 64, (c + 1 + j % 3) % 4)

    for i, (line, rows) in enumerate(
        ((xs_line, xs_rows), (xt_line, xt_rows), (ys_line, ys_rows), (yt_line, yt_rows))
    ):
        early_copies[i].wait()
        for q in range(line.shape[0] // 128):
            part = line[128 * q : 128 * (q + 1)]
            rows[q : q + 1, :] = part.astype(F32).reshape(1, 128)
        q = line.shape[0] // 128
        rows[q : q + 1, 0:1] = line[128 * q : 128 * q + 1].astype(F32).reshape(1, 1)

    lane1 = lanes((1, 128))

    def pair_weights(src, tgt, q):
        low = src[pl.ds(q, 1), :]
        high = pltpu.roll(jnp.where(lane1 == 0, src[pl.ds(q + 1, 1), :], low), 127, 1)
        row = 96 * q // 128
        off = 96 * q % 128
        line = jnp.where(lane1 >= off, tgt[pl.ds(row, 1), :], tgt[pl.ds(row + 1, 1), :])
        line = pltpu.roll(line, (128 - off) % 128, 1)
        cols = jnp.broadcast_to(line, (128, 128)).T
        t_low, t_high = cols[0:96], cols[1:97]
        shared = jnp.maximum(jnp.minimum(high, t_high) - jnp.maximum(low, t_low), 0.0)
        return shared / (t_high - t_low)

    wxp[...] = pair_weights(xs_rows, xt_rows, chip)
    wx = wxp[pl.ds(pl.multiple_of(TB * core, 8), TB), :]
    wx = pltpu.roll(wx, 64 * core, 1)
    wxp[0:TB, :] = wx
    third = wxp[pl.ds(pl.multiple_of(24 * half, 8), 24), :]
    none = jnp.zeros((TB, 128), F32)
    wx = jnp.concatenate(
        [
            jnp.concatenate([wx, pltpu.roll(wx, 64, 1), none[0:32]], axis=0),
            jnp.concatenate([none, none, third, none[0:8]], axis=0),
        ],
        axis=1,
    )[:, 0:192]
    hi, lo = split(wx)
    wx_all[...] = jnp.concatenate([hi, hi, lo], axis=1)

    for copy in early_copies[4:]:
        copy.wait()
    acc[...] = jnp.zeros_like(acc)

    def fold(a):
        out = a[:, 0:128]
        for i in range(1, 6):
            out = out + a[:, 128 * i : 128 * (i + 1)]
        return out

    def rows_of(a):
        return jnp.sum(a, axis=0, keepdims=True)

    lane8 = lanes((8, 768))
    row8 = lax.broadcasted_iota(jnp.int32, (8, 768), 0)
    square = jnp.zeros((8, 768), F32)
    rough = jnp.zeros((8, 768), F32)
    for g in range(6):
        a = [bx[zl, 8 + 8 * g : 16 + 8 * g, :] for zl in range(2)]
        d = a[0] - a[1]
        rough = rough + d * d
        for zl in range(2):
            square = square + a[zl] * a[zl]
            d = jnp.where(lane8 == 0, 0.0, a[zl] - pltpu.roll(a[zl], 1, 1))
            rough = rough + d * d
            if g > 0:
                d = a[zl] - bx[zl, 7 + 8 * g : 15 + 8 * g, :]
            else:
                d = jnp.where(row8 == 0, 0.0, a[zl] - pltpu.roll(a[zl], 1, 0))
            rough = rough + d * d
    tile_a[0, 0:1, :] = rows_of(fold(square))
    tile_a[0, 1:2, :] = rows_of(fold(rough))

    lane48 = lanes((TB, 128))

    def rim_copies(i):
        up, down = (r + 63) % 64, (r + 1) % 64
        left, right = (c + 3) % 4, (c + 1) % 4
        def copy(src, dst, d, peer):
            return pltpu.make_async_remote_copy(
                src_ref=src, dst_ref=dst, send_sem=hs_sem.at[i, d], recv_sem=hr_sem.at[i, d],
                device_id=peer, device_id_type=MESH,
            )
        return (
            copy(hs_row.at[i, 0], hr_row.at[i, 0], 0, (down, c)),
            copy(hs_row.at[i, 1], hr_row.at[i, 1], 1, (up, c)),
            copy(hs_col.at[i, 0], hr_col.at[i, 0], 2, (r, right)),
            copy(hs_col.at[i, 1], hr_col.at[i, 1], 3, (r, left)),
        )

    def rim_start(i, f):
        for zl in range(2):
            hs_row[i, 0, zl : zl + 1, :] = f[zl, 55:56, :]
            hs_row[i, 1, zl : zl + 1, :] = f[zl, 8:9, :]
        hs_col[i, 0] = jnp.where(
            lane48 == 127, f[0, 8:56, 640:768], pltpu.roll(f[1, 8:56, 640:768], 127, 1)
        )
        hs_col[i, 1] = jnp.where(lane48 == 0, f[0, 8:56, 0:128], pltpu.roll(f[1, 8:56, 0:128], 1, 1))
        for copy in rim_copies(i):
            copy.start()

    def rim_wait(i, f):
        for copy in rim_copies(i):
            copy.wait()
        for zl in range(2):
            f[zl, 7:8, :] = hr_row[i, 0, zl : zl + 1, :]
            f[zl, 56:57, :] = hr_row[i, 1, zl : zl + 1, :]

    spot_a = r % 16
    spot_b = y * 4 + c

    def sum_copy(i, stage, j):
        if stage == 0:
            peer = (16 * y + (spot_a + j) % 16, c)
            src, dst = tile_a.at[i], got_a.at[i, spot_a]
        else:
            other = (spot_b + j) % 16
            peer = (16 * (other // 4) + spot_a, other % 4)
            src, dst = tile_b.at[i], got_b.at[i, spot_b]
        return pltpu.make_async_remote_copy(
            src_ref=src, dst_ref=dst, send_sem=ts_sem.at[i, stage], recv_sem=tr_sem.at[i, stage],
            device_id=peer, device_id_type=MESH,
        )

    def sum_start(i, stage):
        @pl.loop(1, 16)
        def _(j):
            sum_copy(i, stage, j).start()

    def sum_wait(i, stage):
        got = got_a if stage == 0 else got_b
        tile = tile_a if stage == 0 else tile_b
        spot = spot_a if stage == 0 else spot_b
        got[i, pl.ds(spot, 1)] = tile[i][None]
        landed = got.at[i, 0:15]
        pltpu.make_async_copy(landed, landed, tr_sem.at[i, stage]).wait()
        total = got[i, 0]
        for j in range(1, 16):
            total = total + got[i, j]
        return total

    def weights_y(k):
        dy, dz = offsets(k, c)
        wh, wl = split(pair_weights(ys_rows, yt_rows, ((y + dy) % 4) * 8 + (z + dz) % 8))
        return jnp.concatenate([wh, wh, wl], axis=1)

    def compute(i):
        steps = [GROUP * i + j for j in range(GROUP)]
        for k in steps:
            fetch(k).wait()
        wy = [weights_y(k) for k in steps]
        cells = [fbuf[k] for k in steps]
        for f in cells:
            for p in range(3):
                acc[p] = acc[p] + jnp.sum(f[p].reshape(8, 8, 128), axis=0)
        outs = []
        for f, w in zip(cells, wy):
            fh, fl = split(f.reshape(192, 128))
            g = dot(wx_all[...], jnp.concatenate([fh, fl, fh], axis=0), ((1,), (0,)))
            gh, gl = split(g)
            outs.append(dot(w, jnp.concatenate([gh, gl, gh], axis=1), ((1,), (1,))))
        for k, out in zip(steps, outs):
            sbuf[2 * k] = out[0:TB]
            sbuf[2 * k + 1] = out[TB : 2 * TB]

    slot = c * 16 + z * 2 + core

    def deliver(src, row, col):
        mine = jnp.logical_and(row == r, col == c)

        @pl.when(mine)
        def _():
            pltpu.make_async_copy(src, rb2.at[slot], rsem2.at[slot]).start()

        @pl.when(jnp.logical_not(mine))
        def _():
            pltpu.make_async_remote_copy(
                src_ref=src, dst_ref=rb2.at[slot], send_sem=ssem2, recv_sem=rsem2.at[slot],
                device_id=(row, col), device_id_type=MESH,
            ).start()

    def send(k):
        dy, dz = offsets(k, c)
        for s in range(2):
            chunk = sbuf.at[2 * k + s]

            @pl.when(dy == 0)
            def _():
                deliver(chunk, 16 * y + (z + dz) % 8 * 2 + s, y)

            @pl.when(dy != 0)
            def _():
                pltpu.make_async_remote_copy(
                    src_ref=chunk, dst_ref=rb1.at[2 * k + s],
                    send_sem=ssem, recv_sem=rsem1.at[2 * k + s],
                    device_id=((r + 16 * dy) % 64, c), device_id_type=MESH,
                ).start()

    def forward(k):
        dy, dz = offsets(k, c)

        @pl.when(dy != 0)
        def _():
            for s in range(2):
                chunk = rb1.at[2 * k + s]
                pltpu.make_async_copy(chunk, chunk, rsem1.at[2 * k + s]).wait()
                deliver(chunk, 16 * y + (z + dz) % 8 * 2 + s, (y - dy + 4) % 4)

    def merge(k):
        cs = (y - k // 2 - c + 32) % 4
        zs = (z - offsets(k, c)[1] + 8) % 8
        for s in range(2):
            block = zs * 2 + s
            place = cs * 16 + block
            got = rb2.at[place]
            pltpu.make_async_copy(got, got, rsem2.at[place]).wait()
            chunk = rb2[place]
            for p in range(3):
                width = TB if p < 2 else 24
                pos = TB * block + (24 * (cs % 2) if p == 2 else 0)
                t0 = pos // 128
                off = pos % 128
                t1 = jnp.minimum(t0 + 1, 5)
                turned = pltpu.roll(chunk, (off + 256 - TB * p) % 128, 1)
                m = (cs // 2) * M + 3 * (cs % 2) + p
                here = pl.ds(pl.multiple_of(t0 * 128, 128), 128)
                inside = jnp.logical_and(lane48 >= off, lane48 < off + width)
                R[m, :, here] = jnp.where(inside, turned, R[m, :, here])
                there = pl.ds(pl.multiple_of(t1 * 128, 128), 128)
                R[m, :, there] = jnp.where(lane48 < off + width - 128, turned, R[m, :, there])

    @pl.loop(0, NQ // GROUP)
    def _(i):
        compute(i)

    hf = half.astype(F32)
    for p in range(3):
        v = rows_of(acc[p])
        tile_a[0, 2 + p : 3 + p, :] = v * (1.0 - hf)
        tile_a[0, 5 + p : 6 + p, :] = v * hf

    pl.semaphore_wait(barrier, 77)

    @pl.loop(0, WINDOW)
    def _(k):
        send(k)

    rim_start(0, bx)
    sum_start(0, 0)

    @pl.loop(0, NQ + LAG_MERGE)
    def _(it):
        @pl.when(it < NQ)
        def _():
            forward(it)

        @pl.when(it < NQ - WINDOW)
        def _():
            send(it + WINDOW)

        @pl.when(it == 10)
        def _():
            tile_b[0] = sum_wait(0, 0)
            sum_start(0, 1)

        @pl.when(it >= LAG_MERGE)
        def _():
            merge(it - LAG_MERGE)

    param = [16.0 / jnp.full((1, 128), table[i].astype(F32)) for i in range(M)]
    param += [jnp.full((1, 128), capacity[i]) for i in range(M)]

    for t in range(6):
        at = slice(128 * t, 128 * (t + 1))
        low = lax.rem(lanes((1, 128)) + 128 * t, TB) < 24
        for zl in range(2):
            m = [R[M * zl + i, :, at] for i in range(M)]
            rest = 1.0 - (m[0] + m[1] + m[3] + m[4])
            m[2], m[5] = jnp.where(low, m[2], rest - m[5]), jnp.where(low, rest - m[2], m[5])
            R[M * zl + 2, :, at] = m[2]
            R[M * zl + 5, :, at] = m[5]
            inverse = m[0] * param[0]
            heat = m[0] * param[M]
            for i in range(1, M):
                inverse = inverse + m[i] * param[i]
                heat = heat + m[i] * param[M + i]
            ix[zl, 8:56, at] = inverse
            cc[zl, :, at] = heat
    rim_start(1, ix)
    rim_wait(0, bx)

    param = [a[:, 0:1] for a in param]
    early = jnp.sum(sum_wait(0, 1), axis=1, keepdims=True)
    norm = early[0:1]
    weight = early[2:3]
    mean_c = early[2:3] * param[M]
    mean_i = early[2:3] * param[0]
    for i in range(1, M):
        weight = weight + early[2 + i : 3 + i]
        mean_c = mean_c + early[2 + i : 3 + i] * param[M + i]
        mean_i = mean_i + early[2 + i : 3 + i] * param[i]
    sigma = mean_c / weight + early[1:2] / norm * weight / mean_i
    per = 1.0 / sigma

    def beside(i, f, zl, g):
        w = f[zl, 8 + 8 * g : 16 + 8 * g, :]
        above = f[zl, 7 + 8 * g : 15 + 8 * g, :]
        below = f[zl, 9 + 8 * g : 17 + 8 * g, :]
        lane = lanes((8, 128))
        hl = pltpu.roll(hr_col[i, 0, 8 * g : 8 * g + 8, :], 1 + zl, 1)
        hr = pltpu.roll(hr_col[i, 1, 8 * g : 8 * g + 8, :], 127 - zl, 1)
        left = pltpu.roll(w, 1, 1)
        right = pltpu.roll(w, 767, 1)
        left = jnp.concatenate([jnp.where(lane == 0, hl, left[:, 0:128]), left[:, 128:]], axis=1)
        right = jnp.concatenate(
            [right[:, 0:640], jnp.where(lane == 127, hr, right[:, 640:])], axis=1
        )
        return w, above, below, left, right

    def apply(i, f, out, out_row):
        odd = jnp.zeros((8, 768), F32)
        even = jnp.zeros((8, 768), F32)
        for zl in range(2):
            for g in range(6):
                at = slice(8 * g, 8 * g + 8)
                w, above, below, left, right = beside(i, f, zl, g)
                other = f[1 - zl, 8 + 8 * g : 16 + 8 * g, :]
                v = cc[zl, at, :] * w
                v = v + fz[at, :] * (w - other)
                v = v + fu[zl, at, :] * (w - above) + fd[zl, at, :] * (w - below)
                v = v + fl[zl, at, :] * (w - left) + fr[zl, at, :] * (w - right)
                out[zl, out_row + 8 * g : out_row + 8 * g + 8, :] = v
                odd = odd + w * v
                even = even + v * v
        return rows_of(fold(odd)), rows_of(fold(even))

    rim_wait(1, ix)
    zero, one = jnp.float32(0.0), jnp.float32(1.0)
    top = jnp.where(r == 0, zero, one)
    bottom = jnp.where(r == 63, zero, one)
    first = jnp.where(c == 0, zero, one)
    last = jnp.where(c == 3, zero, one)
    twice = jnp.broadcast_to(2.0 * per, (8, 768))
    for zl in range(2):
        for g in range(6):
            at = slice(8 * g, 8 * g + 8)
            w, above, below, left, right = beside(1, ix, zl, g)
            f = twice / (w + above)
            fu[zl, at, :] = f * jnp.where(row8 == 0, top, one) if g == 0 else f
            f = twice / (w + below)
            fd[zl, at, :] = f * jnp.where(row8 == 7, bottom, one) if g == 5 else f
            fl[zl, at, :] = twice / (w + left) * jnp.where(lane8 == 0, first, one)
            fr[zl, at, :] = twice / (w + right) * jnp.where(lane8 == 767, last, one)
            if zl == 0:
                fz[at, :] = twice / (w + ix[1, 8 + 8 * g : 16 + 8 * g, :])
            cc[zl, at, :] = cc[zl, at, :] * per - 1.0

    tile_a[1] = jnp.zeros((8, 128), F32)
    s1, s2 = apply(0, bx, v1, 8)
    rim_start(2, v1)
    tile_a[1, 0:1, :] = s1
    tile_a[1, 1:2, :] = s2
    rim_wait(2, v1)
    s1, s2 = apply(2, v1, v2, 8)
    rim_start(3, v2)
    tile_a[1, 2:3, :] = s1
    tile_a[1, 3:4, :] = s2
    rim_wait(3, v2)
    s1, s2 = apply(3, v2, v3, 0)
    tile_a[1, 4:5, :] = s1
    sum_start(1, 0)
    tile_b[1] = sum_wait(1, 0)
    sum_start(1, 1)
    sums = jnp.sum(sum_wait(1, 1), axis=1, keepdims=True)
    mom = [norm] + [sums[i : i + 1] for i in range(5)]

    def inner(p, q):
        total = None
        for i, pi in enumerate(p):
            for j, qj in enumerate(q):
                term = pi * qj * mom[i + j]
                total = term if total is None else total + term
        return total

    def combine(p, q, s):
        size = max(len(p), len(q))
        out = []
        for i in range(size):
            if i < len(p) and i < len(q):
                out.append(p[i] + s * q[i])
            else:
                out.append(p[i] if i < len(p) else s * q[i])
        return out

    unit = jnp.ones((1, 1), F32)
    x, res, direction, rr = [], [unit], [unit], norm
    for it in range(3):
        n = len(direction)
        applied = [direction[0] * sigma]
        applied += [(direction[i] + direction[i - 1]) * sigma for i in range(1, n)]
        applied += [direction[n - 1] * sigma]
        alpha = rr / inner(direction, applied)
        x = combine(x, direction, alpha)
        res = combine(res, applied, -alpha)
        if it < 2:
            new = inner(res, res)
            direction = combine(res, direction, new / rr)
            rr = new

    for zl in range(2):
        for g in range(6):
            at = slice(8 * g, 8 * g + 8)
            ext = slice(8 + 8 * g, 16 + 8 * g)
            base = (bx[zl, ext, :], v1[zl, ext, :], v2[zl, ext, :], v3[zl, at, :])
            out = x[0] * base[0]
            for i in range(1, 3):
                out = out + x[i] * base[i]
            x_out[zl, at, :] = out
            out = res[0] * base[0]
            for i in range(1, 4):
                out = out + res[i] * base[i]
            r_out[zl, at, :] = out

    sent = sbuf.at[0:48]
    pltpu.make_async_copy(sent, sent, ssem).wait()
    sent = rb2.at[0:63]
    pltpu.make_async_copy(sent, sent, ssem2).wait()
    for i in range(2):
        for stage in range(2):
            sent = got_a.at[i, 0:15]
            pltpu.make_async_copy(sent, sent, ts_sem.at[i, stage]).wait()


def put_out(*refs):
    sem = refs[6]
    copies = [pltpu.make_async_copy(refs[i], refs[3 + i], sem.at[i]) for i in range(3)]
    for copy in copies:
        copy.start()
    for copy in copies:
        copy.wait()


def per_device(
    fractions_source,
    x_source_edges,
    x_target_edges,
    y_source_edges,
    y_target_edges,
    conductivity_table,
    capacity,
    thermal_source_term,
):
    field = jax.ShapeDtypeStruct((2, TB, 768), F32)
    vmem = pl.BlockSpec(memory_space=pltpu.VMEM)
    hbm = pl.BlockSpec(memory_space=pltpu.HBM)
    shapes = (jax.ShapeDtypeStruct((2 * M, TB, 768), F32), field, field)
    ext = VM((2, 64, 768), F32)
    inner = VM((2, TB, 768), F32)
    made = pl.pallas_call(
        kernel,
        out_shape=shapes,
        in_specs=[hbm] * 8,
        out_specs=(vmem, vmem, vmem),
        scratch_shapes=[
            VM((4097,), jnp.int32), VM((3073,), jnp.int32),
            VM((4097,), jnp.int32), VM((3073,), jnp.int32),
            VM((40, 128), F32), VM((32, 128), F32), VM((40, 128), F32), VM((32, 128), F32),
            pltpu.SMEM((M,), jnp.int32), pltpu.SMEM((M,), F32),
            VM((NQ, 3, 64, 128), F32),
            VM((96, 128), F32),
            VM((128, 576), BF16),
            VM((64, TB, 128), F32), VM((64, TB, 128), F32), VM((64, TB, 128), F32),
            ext, ext, ext, ext, inner, inner,
            inner, inner, inner, inner, VM((TB, 768), F32),
            VM((4, 2, 2, 768), F32), VM((4, 2, 2, 768), F32),
            VM((4, 2, TB, 128), F32), VM((4, 2, TB, 128), F32),
            VM((3, 8, 128), F32),
            VM((2, 8, 128), F32), VM((2, 16, 8, 128), F32),
            VM((2, 8, 128), F32), VM((2, 16, 8, 128), F32),
            DMA((7,)), DMA((NQ,)), DMA, DMA((64,)), DMA, DMA((64,)),
            DMA((4, 4)), DMA((4, 4)), DMA((2, 2)), DMA((2, 2)),
        ],
        compiler_params=pltpu.CompilerParams(
            collective_id=0, has_side_effects=True, vmem_limit_bytes=48 * 2**20
        ),
    )(
        *[
            pltpu.with_memory_space_constraint(a, pltpu.HBM)
            for a in (
                fractions_source, x_source_edges, x_target_edges, y_source_edges, y_target_edges,
                conductivity_table, capacity, thermal_source_term,
            )
        ]
    )
    return pl.pallas_call(
        put_out,
        out_shape=shapes,
        in_specs=[pl.BlockSpec(memory_space=pl.ANY)] * 3,
        out_specs=(hbm, hbm, hbm),
        scratch_shapes=[DMA((3,))],
        compiler_params=pltpu.CompilerParams(vmem_limit_bytes=2**20),
    )(*made)


def solution(mesh):
    placed = (P("col", "row", None), P(), P(), P(), P(), P(), P(), P(None, "row", "col"))
    return jax.shard_map(
        per_device,
        mesh=mesh,
        in_specs=placed,
        out_specs=(P(None, "row", "col"), P(None, "row", "col"), P(None, "row", "col")),
        check_vma=False,
    )
```

```python
import jax
import jax.numpy as jnp
from jax import lax
from jax.experimental import pallas as pl
from jax.experimental.pallas import tpu as pltpu
from jax.sharding import PartitionSpec as P

M = 6
TB = 48
NQ = 32
GROUP = 4
AHEAD = 12
WINDOW = 12
LAG_MERGE = 16
MESH = pl.DeviceIdType.MESH
F32 = jnp.float32
BF16 = jnp.bfloat16
VM = pltpu.VMEM
DMA = pltpu.SemaphoreType.DMA


def split(a):
    high = a.astype(BF16)
    return high, (a - high.astype(F32)).astype(BF16)


def dot(a, b, dims):
    return lax.dot_general(a, b, (dims, ((), ())), preferred_element_type=F32)


def offsets(k, c):
    g, s = k // 8, k % 2
    dz = jnp.where(s == 0, 4 - g, jnp.where(g == 0, 0, 4 + g))
    return (k // 2 + c) % 4, dz


def lanes(shape):
    return lax.broadcasted_iota(jnp.int32, shape, len(shape) - 1)


def kernel(
    frac, xs_edges, xt_edges, ys_edges, yt_edges, table_in, capacity_in, b_ref, R, x_out, r_out,
    xs_line, xt_line, ys_line, yt_line, xs_rows, xt_rows, ys_rows, yt_rows,
    table, capacity, fbuf, wxp, wx_all, sbuf, rb1, rb2, bx, ix, v1, v2, v3, cc,
    fu, fd, fl, fr, fz, hs_row, hr_row, hs_col, hr_col, acc, tile_a, got_a, tile_b, got_b,
    esem, fsem, ssem, rsem1, ssem2, rsem2, hs_sem, hr_sem, ts_sem, tr_sem,
):
    r = lax.axis_index("row")
    c = lax.axis_index("col")
    core = r % 2
    chip = r // 2
    y, z = chip // 8, chip % 8
    half = c % 2

    lines = ((xs_edges, xs_line), (xt_edges, xt_line), (ys_edges, ys_line), (yt_edges, yt_line))
    early_copies = [pltpu.make_async_copy(a, b, esem.at[i]) for i, (a, b) in enumerate(lines)]
    early_copies.append(pltpu.make_async_copy(b_ref, bx.at[:, 8:56, :], esem.at[4]))
    early_copies.append(pltpu.make_async_copy(table_in, table, esem.at[5]))
    early_copies.append(pltpu.make_async_copy(capacity_in, capacity, esem.at[6]))
    for copy in early_copies:
        copy.start()

    def fetch(k):
        dy, dz = offsets(k, c)
        q = ((y + dy) % 4) * 8 + (z + dz) % 8
        return pltpu.make_async_copy(
            frac.at[:, :, pl.ds(pl.multiple_of(q * 128, 128), 128)], fbuf.at[k], fsem.at[k]
        )

    @pl.loop(0, NQ)
    def _(k):
        fetch(k).start()

    barrier = pltpu.get_barrier_semaphore()

    def greet(row, col):
        pl.semaphore_signal(barrier, inc=1, device_id=(row, col), device_id_type=MESH)

    @pl.loop(1, 64)
    def _(j):
        greet(16 * y + (r + j // 4) % 16, (c + j % 4) % 4)

    @pl.loop(1, 4)
    def _(j):
        greet((r + 16 * j) % 64, c)

    greet((r + 1) % 64, c)
    greet((r + 63) % 64, c)

    @pl.loop(0, 9)
    def _(j):
        greet((r + 16 * (1 + j // 3)) % 64, (c + 1 + j % 3) % 4)

    for i, (line, rows) in enumerate(
        ((xs_line, xs_rows), (xt_line, xt_rows), (ys_line, ys_rows), (yt_line, yt_rows))
    ):
        early_copies[i].wait()
        for q in range(line.shape[0] // 128):
            part = line[128 * q : 128 * (q + 1)]
            rows[q : q + 1, :] = part.astype(F32).reshape(1, 128)
        q = line.shape[0] // 128
        rows[q : q + 1, 0:1] = line[128 * q : 128 * q + 1].astype(F32).reshape(1, 1)

    lane1 = lanes((1, 128))

    def pair_weights(src, tgt, q):
        low = src[pl.ds(q, 1), :]
        high = pltpu.roll(jnp.where(lane1 == 0, src[pl.ds(q + 1, 1), :], low), 127, 1)
        row = 96 * q // 128
        off = 96 * q % 128
        line = jnp.where(lane1 >= off, tgt[pl.ds(row, 1), :], tgt[pl.ds(row + 1, 1), :])
        line = pltpu.roll(line, (128 - off) % 128, 1)
        cols = jnp.broadcast_to(line, (128, 128)).T
        t_low, t_high = cols[0:96], cols[1:97]
        shared = jnp.maximum(jnp.minimum(high, t_high) - jnp.maximum(low, t_low), 0.0)
        return shared / (t_high - t_low)

    wxp[...] = pair_weights(xs_rows, xt_rows, chip)
    wx = wxp[pl.ds(pl.multiple_of(TB * core, 8), TB), :]
    wx = pltpu.roll(wx, 64 * core, 1)
    wxp[0:TB, :] = wx
    third = wxp[pl.ds(pl.multiple_of(24 * half, 8), 24), :]
    none = jnp.zeros((TB, 128), F32)
    wx = jnp.concatenate(
        [
            jnp.concatenate([wx, pltpu.roll(wx, 64, 1), none[0:32]], axis=0),
            jnp.concatenate([none, none, third, none[0:8]], axis=0),
        ],
        axis=1,
    )[:, 0:192]
    hi, lo = split(wx)
    wx_all[...] = jnp.concatenate([hi, hi, lo], axis=1)

    for copy in early_copies[4:]:
        copy.wait()
    acc[...] = jnp.zeros_like(acc)

    def fold(a):
        out = a[:, 0:128]
        for i in range(1, 6):
            out = out + a[:, 128 * i : 128 * (i + 1)]
        return out

    def rows_of(a):
        return jnp.sum(a, axis=0, keepdims=True)

    lane8 = lanes((8, 768))
    row8 = lax.broadcasted_iota(jnp.int32, (8, 768), 0)
    square = jnp.zeros((8, 768), F32)
    rough = jnp.zeros((8, 768), F32)
    for g in range(6):
        a = [bx[zl, 8 + 8 * g : 16 + 8 * g, :] for zl in range(2)]
        d = a[0] - a[1]
        rough = rough + d * d
        for zl in range(2):
            square = square + a[zl] * a[zl]
            d = jnp.where(lane8 == 0, 0.0, a[zl] - pltpu.roll(a[zl], 1, 1))
            rough = rough + d * d
            if g > 0:
                d = a[zl] - bx[zl, 7 + 8 * g : 15 + 8 * g, :]
            else:
                d = jnp.where(row8 == 0, 0.0, a[zl] - pltpu.roll(a[zl], 1, 0))
            rough = rough + d * d
    tile_a[0, 0:1, :] = rows_of(fold(square))
    tile_a[0, 1:2, :] = rows_of(fold(rough))

    lane48 = lanes((TB, 128))

    def rim_copies(i):
        up, down = (r + 63) % 64, (r + 1) % 64
        left, right = (c + 3) % 4, (c + 1) % 4
        def copy(src, dst, d, peer):
            return pltpu.make_async_remote_copy(
                src_ref=src, dst_ref=dst, send_sem=hs_sem.at[i, d], recv_sem=hr_sem.at[i, d],
                device_id=peer, device_id_type=MESH,
            )
        return (
            copy(hs_row.at[i, 0], hr_row.at[i, 0], 0, (down, c)),
            copy(hs_row.at[i, 1], hr_row.at[i, 1], 1, (up, c)),
            copy(hs_col.at[i, 0], hr_col.at[i, 0], 2, (r, right)),
            copy(hs_col.at[i, 1], hr_col.at[i, 1], 3, (r, left)),
        )

    def rim_start(i, f):
        for zl in range(2):
            hs_row[i, 0, zl : zl + 1, :] = f[zl, 55:56, :]
            hs_row[i, 1, zl : zl + 1, :] = f[zl, 8:9, :]
        hs_col[i, 0] = jnp.where(
            lane48 == 127, f[0, 8:56, 640:768], pltpu.roll(f[1, 8:56, 640:768], 127, 1)
        )
        hs_col[i, 1] = jnp.where(lane48 == 0, f[0, 8:56, 0:128], pltpu.roll(f[1, 8:56, 0:128], 1, 1))
        for copy in rim_copies(i):
            copy.start()

    def rim_wait(i, f):
        for copy in rim_copies(i):
            copy.wait()
        for zl in range(2):
            f[zl, 7:8, :] = hr_row[i, 0, zl : zl + 1, :]
            f[zl, 56:57, :] = hr_row[i, 1, zl : zl + 1, :]

    spot_a = r % 16
    spot_b = y * 4 + c

    def sum_copy(i, stage, j):
        if stage == 0:
            peer = (16 * y + (spot_a + j) % 16, c)
            src, dst = tile_a.at[i], got_a.at[i, spot_a]
        else:
            other = (spot_b + j) % 16
            peer = (16 * (other // 4) + spot_a, other % 4)
            src, dst = tile_b.at[i], got_b.at[i, spot_b]
        return pltpu.make_async_remote_copy(
            src_ref=src, dst_ref=dst, send_sem=ts_sem.at[i, stage], recv_sem=tr_sem.at[i, stage],
            device_id=peer, device_id_type=MESH,
        )

    def sum_start(i, stage):
        @pl.loop(1, 16)
        def _(j):
            sum_copy(i, stage, j).start()

    def sum_wait(i, stage):
        got = got_a if stage == 0 else got_b
        tile = tile_a if stage == 0 else tile_b
        spot = spot_a if stage == 0 else spot_b
        got[i, pl.ds(spot, 1)] = tile[i][None]
        landed = got.at[i, 0:15]
        pltpu.make_async_copy(landed, landed, tr_sem.at[i, stage]).wait()
        total = got[i, 0]
        for j in range(1, 16):
            total = total + got[i, j]
        return total

    def weights_y(k):
        dy, dz = offsets(k, c)
        wh, wl = split(pair_weights(ys_rows, yt_rows, ((y + dy) % 4) * 8 + (z + dz) % 8))
        return jnp.concatenate([wh, wh, wl], axis=1)

    def compute(i):
        steps = [GROUP * i + j for j in range(GROUP)]
        for k in steps:
            fetch(k).wait()
        wy = [weights_y(k) for k in steps]
        cells = [fbuf[k] for k in steps]
        for f in cells:
            for p in range(3):
                acc[p] = acc[p] + jnp.sum(f[p].reshape(8, 8, 128), axis=0)
        outs = []
        for f, w in zip(cells, wy):
            fh, fl = split(f.reshape(192, 128))
            g = dot(wx_all[...], jnp.concatenate([fh, fl, fh], axis=0), ((1,), (0,)))
            gh, gl = split(g)
            outs.append(dot(w, jnp.concatenate([gh, gl, gh], axis=1), ((1,), (1,))))
        for k, out in zip(steps, outs):
            sbuf[2 * k] = out[0:TB]
            sbuf[2 * k + 1] = out[TB : 2 * TB]

    slot = c * 16 + z * 2 + core

    def deliver(src, row, col):
        mine = jnp.logical_and(row == r, col == c)

        @pl.when(mine)
        def _():
            pltpu.make_async_copy(src, rb2.at[slot], rsem2.at[slot]).start()

        @pl.when(jnp.logical_not(mine))
        def _():
            pltpu.make_async_remote_copy(
                src_ref=src, dst_ref=rb2.at[slot], send_sem=ssem2, recv_sem=rsem2.at[slot],
                device_id=(row, col), device_id_type=MESH,
            ).start()

    def send(k):
        dy, dz = offsets(k, c)
        for s in range(2):
            chunk = sbuf.at[2 * k + s]

            @pl.when(dy == 0)
            def _():
                deliver(chunk, 16 * y + (z + dz) % 8 * 2 + s, y)

            @pl.when(dy != 0)
            def _():
                pltpu.make_async_remote_copy(
                    src_ref=chunk, dst_ref=rb1.at[2 * k + s],
                    send_sem=ssem, recv_sem=rsem1.at[2 * k + s],
                    device_id=((r + 16 * dy) % 64, c), device_id_type=MESH,
                ).start()

    def forward(k):
        dy, dz = offsets(k, c)

        @pl.when(dy != 0)
        def _():
            for s in range(2):
                chunk = rb1.at[2 * k + s]
                pltpu.make_async_copy(chunk, chunk, rsem1.at[2 * k + s]).wait()
                deliver(chunk, 16 * y + (z + dz) % 8 * 2 + s, (y - dy + 4) % 4)

    def merge(k):
        cs = (y - k // 2 - c + 32) % 4
        zs = (z - offsets(k, c)[1] + 8) % 8
        for s in range(2):
            block = zs * 2 + s
            place = cs * 16 + block
            got = rb2.at[place]
            pltpu.make_async_copy(got, got, rsem2.at[place]).wait()
            chunk = rb2[place]
            for p in range(3):
                width = TB if p < 2 else 24
                pos = TB * block + (24 * (cs % 2) if p == 2 else 0)
                t0 = pos // 128
                off = pos % 128
                t1 = jnp.minimum(t0 + 1, 5)
                turned = pltpu.roll(chunk, (off + 256 - TB * p) % 128, 1)
                m = (cs // 2) * M + 3 * (cs % 2) + p
                here = pl.ds(pl.multiple_of(t0 * 128, 128), 128)
                inside = jnp.logical_and(lane48 >= off, lane48 < off + width)
                R[m, :, here] = jnp.where(inside, turned, R[m, :, here])
                there = pl.ds(pl.multiple_of(t1 * 128, 128), 128)
                R[m, :, there] = jnp.where(lane48 < off + width - 128, turned, R[m, :, there])

    @pl.loop(0, AHEAD // GROUP)
    def _(i):
        compute(i)

    pl.semaphore_wait(barrier, 77)

    @pl.loop(0, WINDOW)
    def _(k):
        send(k)

    rim_start(0, bx)

    @pl.loop(0, NQ + LAG_MERGE)
    def _(it):
        @pl.when(jnp.logical_and(it < NQ - AHEAD, it % GROUP == 0))
        def _():
            compute((it + AHEAD) // GROUP)

        @pl.when(it == NQ - AHEAD)
        def _():
            hf = half.astype(F32)
            for p in range(3):
                v = rows_of(acc[p])
                tile_a[0, 2 + p : 3 + p, :] = v * (1.0 - hf)
                tile_a[0, 5 + p : 6 + p, :] = v * hf
            sum_start(0, 0)

        @pl.when(it < NQ)
        def _():
            forward(it)

        @pl.when(it < NQ - WINDOW)
        def _():
            send(it + WINDOW)

        @pl.when(it == NQ - AHEAD + 8)
        def _():
            tile_b[0] = sum_wait(0, 0)
            sum_start(0, 1)

        @pl.when(it >= LAG_MERGE)
        def _():
            merge(it - LAG_MERGE)

    param = [16.0 / jnp.full((1, 128), table[i].astype(F32)) for i in range(M)]
    param += [jnp.full((1, 128), capacity[i]) for i in range(M)]

    for t in range(6):
        at = slice(128 * t, 128 * (t + 1))
        low = lax.rem(lanes((1, 128)) + 128 * t, TB) < 24
        for zl in range(2):
            m = [R[M * zl + i, :, at] for i in range(M)]
            rest = 1.0 - (m[0] + m[1] + m[3] + m[4])
            m[2], m[5] = jnp.where(low, m[2], rest - m[5]), jnp.where(low, rest - m[2], m[5])
            R[M * zl + 2, :, at] = m[2]
            R[M * zl + 5, :, at] = m[5]
            inverse = m[0] * param[0]
            heat = m[0] * param[M]
            for i in range(1, M):
                inverse = inverse + m[i] * param[i]
                heat = heat + m[i] * param[M + i]
            ix[zl, 8:56, at] = inverse
            cc[zl, :, at] = heat
    rim_start(1, ix)
    rim_wait(0, bx)

    param = [a[:, 0:1] for a in param]
    early = jnp.sum(sum_wait(0, 1), axis=1, keepdims=True)
    norm = early[0:1]
    weight = early[2:3]
    mean_c = early[2:3] * param[M]
    mean_i = early[2:3] * param[0]
    for i in range(1, M):
        weight = weight + early[2 + i : 3 + i]
        mean_c = mean_c + early[2 + i : 3 + i] * param[M + i]
        mean_i = mean_i + early[2 + i : 3 + i] * param[i]
    sigma = mean_c / weight + early[1:2] / norm * weight / mean_i
    per = 1.0 / sigma

    def beside(i, f, zl, g):
        w = f[zl, 8 + 8 * g : 16 + 8 * g, :]
        above = f[zl, 7 + 8 * g : 15 + 8 * g, :]
        below = f[zl, 9 + 8 * g : 17 + 8 * g, :]
        lane = lanes((8, 128))
        hl = pltpu.roll(hr_col[i, 0, 8 * g : 8 * g + 8, :], 1 + zl, 1)
        hr = pltpu.roll(hr_col[i, 1, 8 * g : 8 * g + 8, :], 127 - zl, 1)
        left = pltpu.roll(w, 1, 1)
        right = pltpu.roll(w, 767, 1)
        left = jnp.concatenate([jnp.where(lane == 0, hl, left[:, 0:128]), left[:, 128:]], axis=1)
        right = jnp.concatenate(
            [right[:, 0:640], jnp.where(lane == 127, hr, right[:, 640:])], axis=1
        )
        return w, above, below, left, right

    def apply(i, f, out, out_row):
        odd = jnp.zeros((8, 768), F32)
        even = jnp.zeros((8, 768), F32)
        for zl in range(2):
            for g in range(6):
                at = slice(8 * g, 8 * g + 8)
                w, above, below, left, right = beside(i, f, zl, g)
                other = f[1 - zl, 8 + 8 * g : 16 + 8 * g, :]
                v = cc[zl, at, :] * w
                v = v + fz[at, :] * (w - other)
                v = v + fu[zl, at, :] * (w - above) + fd[zl, at, :] * (w - below)
                v = v + fl[zl, at, :] * (w - left) + fr[zl, at, :] * (w - right)
                out[zl, out_row + 8 * g : out_row + 8 * g + 8, :] = v
                odd = odd + w * v
                even = even + v * v
        return rows_of(fold(odd)), rows_of(fold(even))

    rim_wait(1, ix)
    zero, one = jnp.float32(0.0), jnp.float32(1.0)
    top = jnp.where(r == 0, zero, one)
    bottom = jnp.where(r == 63, zero, one)
    first = jnp.where(c == 0, zero, one)
    last = jnp.where(c == 3, zero, one)
    twice = jnp.broadcast_to(2.0 * per, (8, 768))
    for zl in range(2):
        for g in range(6):
            at = slice(8 * g, 8 * g + 8)
            w, above, below, left, right = beside(1, ix, zl, g)
            f = twice / (w + above)
            fu[zl, at, :] = f * jnp.where(row8 == 0, top, one) if g == 0 else f
            f = twice / (w + below)
            fd[zl, at, :] = f * jnp.where(row8 == 7, bottom, one) if g == 5 else f
            fl[zl, at, :] = twice / (w + left) * jnp.where(lane8 == 0, first, one)
            fr[zl, at, :] = twice / (w + right) * jnp.where(lane8 == 767, last, one)
            if zl == 0:
                fz[at, :] = twice / (w + ix[1, 8 + 8 * g : 16 + 8 * g, :])
            cc[zl, at, :] = cc[zl, at, :] * per - 1.0

    tile_a[1] = jnp.zeros((8, 128), F32)
    s1, s2 = apply(0, bx, v1, 8)
    rim_start(2, v1)
    tile_a[1, 0:1, :] = s1
    tile_a[1, 1:2, :] = s2
    rim_wait(2, v1)
    s1, s2 = apply(2, v1, v2, 8)
    rim_start(3, v2)
    tile_a[1, 2:3, :] = s1
    tile_a[1, 3:4, :] = s2
    rim_wait(3, v2)
    s1, s2 = apply(3, v2, v3, 0)
    tile_a[1, 4:5, :] = s1
    sum_start(1, 0)
    tile_b[1] = sum_wait(1, 0)
    sum_start(1, 1)
    sums = jnp.sum(sum_wait(1, 1), axis=1, keepdims=True)
    mom = [norm] + [sums[i : i + 1] for i in range(5)]

    def inner(p, q):
        total = None
        for i, pi in enumerate(p):
            for j, qj in enumerate(q):
                term = pi * qj * mom[i + j]
                total = term if total is None else total + term
        return total

    def combine(p, q, s):
        size = max(len(p), len(q))
        out = []
        for i in range(size):
            if i < len(p) and i < len(q):
                out.append(p[i] + s * q[i])
            else:
                out.append(p[i] if i < len(p) else s * q[i])
        return out

    unit = jnp.ones((1, 1), F32)
    x, res, direction, rr = [], [unit], [unit], norm
    for it in range(3):
        n = len(direction)
        applied = [direction[0] * sigma]
        applied += [(direction[i] + direction[i - 1]) * sigma for i in range(1, n)]
        applied += [direction[n - 1] * sigma]
        alpha = rr / inner(direction, applied)
        x = combine(x, direction, alpha)
        res = combine(res, applied, -alpha)
        if it < 2:
            new = inner(res, res)
            direction = combine(res, direction, new / rr)
            rr = new

    for zl in range(2):
        for g in range(6):
            at = slice(8 * g, 8 * g + 8)
            ext = slice(8 + 8 * g, 16 + 8 * g)
            base = (bx[zl, ext, :], v1[zl, ext, :], v2[zl, ext, :], v3[zl, at, :])
            out = x[0] * base[0]
            for i in range(1, 3):
                out = out + x[i] * base[i]
            x_out[zl, at, :] = out
            out = res[0] * base[0]
            for i in range(1, 4):
                out = out + res[i] * base[i]
            r_out[zl, at, :] = out

    sent = sbuf.at[0:48]
    pltpu.make_async_copy(sent, sent, ssem).wait()
    sent = rb2.at[0:63]
    pltpu.make_async_copy(sent, sent, ssem2).wait()
    for i in range(2):
        for stage in range(2):
            sent = got_a.at[i, 0:15]
            pltpu.make_async_copy(sent, sent, ts_sem.at[i, stage]).wait()


def put_out(*refs):
    sem = refs[6]
    copies = [pltpu.make_async_copy(refs[i], refs[3 + i], sem.at[i]) for i in range(3)]
    for copy in copies:
        copy.start()
    for copy in copies:
        copy.wait()


def per_device(
    fractions_source,
    x_source_edges,
    x_target_edges,
    y_source_edges,
    y_target_edges,
    conductivity_table,
    capacity,
    thermal_source_term,
):
    field = jax.ShapeDtypeStruct((2, TB, 768), F32)
    vmem = pl.BlockSpec(memory_space=pltpu.VMEM)
    hbm = pl.BlockSpec(memory_space=pltpu.HBM)
    shapes = (jax.ShapeDtypeStruct((2 * M, TB, 768), F32), field, field)
    ext = VM((2, 64, 768), F32)
    inner = VM((2, TB, 768), F32)
    made = pl.pallas_call(
        kernel,
        out_shape=shapes,
        in_specs=[hbm] * 8,
        out_specs=(vmem, vmem, vmem),
        scratch_shapes=[
            VM((4097,), jnp.int32), VM((3073,), jnp.int32),
            VM((4097,), jnp.int32), VM((3073,), jnp.int32),
            VM((40, 128), F32), VM((32, 128), F32), VM((40, 128), F32), VM((32, 128), F32),
            pltpu.SMEM((M,), jnp.int32), pltpu.SMEM((M,), F32),
            VM((NQ, 3, 64, 128), F32),
            VM((96, 128), F32),
            VM((128, 576), BF16),
            VM((64, TB, 128), F32), VM((64, TB, 128), F32), VM((64, TB, 128), F32),
            ext, ext, ext, ext, inner, inner,
            inner, inner, inner, inner, VM((TB, 768), F32),
            VM((4, 2, 2, 768), F32), VM((4, 2, 2, 768), F32),
            VM((4, 2, TB, 128), F32), VM((4, 2, TB, 128), F32),
            VM((3, 8, 128), F32),
            VM((2, 8, 128), F32), VM((2, 16, 8, 128), F32),
            VM((2, 8, 128), F32), VM((2, 16, 8, 128), F32),
            DMA((7,)), DMA((NQ,)), DMA, DMA((64,)), DMA, DMA((64,)),
            DMA((4, 4)), DMA((4, 4)), DMA((2, 2)), DMA((2, 2)),
        ],
        compiler_params=pltpu.CompilerParams(
            collective_id=0, has_side_effects=True, vmem_limit_bytes=48 * 2**20
        ),
    )(
        *[
            pltpu.with_memory_space_constraint(a, pltpu.HBM)
            for a in (
                fractions_source, x_source_edges, x_target_edges, y_source_edges, y_target_edges,
                conductivity_table, capacity, thermal_source_term,
            )
        ]
    )
    return pl.pallas_call(
        put_out,
        out_shape=shapes,
        in_specs=[pl.BlockSpec(memory_space=pl.ANY)] * 3,
        out_specs=(hbm, hbm, hbm),
        scratch_shapes=[DMA((3,))],
        compiler_params=pltpu.CompilerParams(vmem_limit_bytes=2**20),
    )(*made)


def solution(mesh):
    placed = (P("col", "row", None), P(), P(), P(), P(), P(), P(), P(None, "row", "col"))
    return jax.shard_map(
        per_device,
        mesh=mesh,
        in_specs=placed,
        out_specs=(P(None, "row", "col"), P(None, "row", "col"), P(None, "row", "col")),
        check_vma=False,
    )
```

```python
import jax
import jax.numpy as jnp
from jax import lax
from jax.experimental import pallas as pl
from jax.experimental.pallas import tpu as pltpu
from jax.sharding import PartitionSpec as P

M = 6
TB = 48
NQ = 32
GROUP = 4
AHEAD = 12
WINDOW = 12
LAG_MERGE = 16
MESH = pl.DeviceIdType.MESH
F32 = jnp.float32
BF16 = jnp.bfloat16
VM = pltpu.VMEM
DMA = pltpu.SemaphoreType.DMA
IN = slice(128, 896)


def split(a):
    high = a.astype(BF16)
    return high, (a - high.astype(F32)).astype(BF16)


def dot(a, b, dims):
    return lax.dot_general(a, b, (dims, ((), ())), preferred_element_type=F32)


def offsets(k, c):
    g, s = k // 8, k % 2
    dz = jnp.where(s == 0, 4 - g, jnp.where(g == 0, 0, 4 + g))
    return (k // 2 + c) % 4, dz


def lanes(shape):
    return lax.broadcasted_iota(jnp.int32, shape, len(shape) - 1)


def kernel(
    frac, xs_edges, xt_edges, ys_edges, yt_edges, table_in, capacity_in, b_ref, R, x_out, r_out,
    xs_line, xt_line, ys_line, yt_line, xs_rows, xt_rows, ys_rows, yt_rows,
    table, capacity, fbuf, wxp, wx_all, sbuf, rb1, rb2, bx, ix, v1, v2, v3, cc,
    fu, fl, fz, hs_row, hr_row, hs_col, hr_col, acc, tile_a, got_a, tile_b, got_b,
    esem, fsem, ssem, rsem1, ssem2, rsem2, hs_sem, hr_sem, ts_sem, tr_sem,
):
    r = lax.axis_index("row")
    c = lax.axis_index("col")
    core = r % 2
    chip = r // 2
    y, z = chip // 8, chip % 8
    half = c % 2

    lines = ((xs_edges, xs_line), (xt_edges, xt_line), (ys_edges, ys_line), (yt_edges, yt_line))
    early_copies = [pltpu.make_async_copy(a, b, esem.at[i]) for i, (a, b) in enumerate(lines)]
    early_copies.append(pltpu.make_async_copy(b_ref, bx.at[:, 8:56, IN], esem.at[4]))
    early_copies.append(pltpu.make_async_copy(table_in, table, esem.at[5]))
    early_copies.append(pltpu.make_async_copy(capacity_in, capacity, esem.at[6]))
    for copy in early_copies:
        copy.start()

    def fetch(k):
        dy, dz = offsets(k, c)
        q = ((y + dy) % 4) * 8 + (z + dz) % 8
        return pltpu.make_async_copy(
            frac.at[:, :, pl.ds(pl.multiple_of(q * 128, 128), 128)], fbuf.at[k], fsem.at[k]
        )

    @pl.loop(0, NQ)
    def _(k):
        fetch(k).start()

    barrier = pltpu.get_barrier_semaphore()

    def greet(row, col):
        pl.semaphore_signal(barrier, inc=1, device_id=(row, col), device_id_type=MESH)

    @pl.loop(1, 64)
    def _(j):
        greet(16 * y + (r + j // 4) % 16, (c + j % 4) % 4)

    @pl.loop(1, 4)
    def _(j):
        greet((r + 16 * j) % 64, c)

    for side in (1, 63):
        greet((r + side) % 64, c)
        greet((r + side) % 64, (c + 1) % 4)
        greet((r + side) % 64, (c + 3) % 4)

    @pl.loop(0, 9)
    def _(j):
        greet((r + 16 * (1 + j // 3)) % 64, (c + 1 + j % 3) % 4)

    for i, (line, rows) in enumerate(
        ((xs_line, xs_rows), (xt_line, xt_rows), (ys_line, ys_rows), (yt_line, yt_rows))
    ):
        early_copies[i].wait()
        for q in range(line.shape[0] // 128):
            part = line[128 * q : 128 * (q + 1)]
            rows[q : q + 1, :] = part.astype(F32).reshape(1, 128)
        q = line.shape[0] // 128
        rows[q : q + 1, 0:1] = line[128 * q : 128 * q + 1].astype(F32).reshape(1, 1)

    lane1 = lanes((1, 128))

    def pair_weights(src, tgt, q):
        low = src[pl.ds(q, 1), :]
        high = pltpu.roll(jnp.where(lane1 == 0, src[pl.ds(q + 1, 1), :], low), 127, 1)
        row = 96 * q // 128
        off = 96 * q % 128
        line = jnp.where(lane1 >= off, tgt[pl.ds(row, 1), :], tgt[pl.ds(row + 1, 1), :])
        line = pltpu.roll(line, (128 - off) % 128, 1)
        cols = jnp.broadcast_to(line, (128, 128)).T
        t_low, t_high = cols[0:96], cols[1:97]
        shared = jnp.maximum(jnp.minimum(high, t_high) - jnp.maximum(low, t_low), 0.0)
        return shared / (t_high - t_low)

    wxp[...] = pair_weights(xs_rows, xt_rows, chip)
    wx = wxp[pl.ds(pl.multiple_of(TB * core, 8), TB), :]
    wx = pltpu.roll(wx, 64 * core, 1)
    wxp[0:TB, :] = wx
    third = wxp[pl.ds(pl.multiple_of(24 * half, 8), 24), :]
    none = jnp.zeros((TB, 128), F32)
    wx = jnp.concatenate(
        [
            jnp.concatenate([wx, pltpu.roll(wx, 64, 1), none[0:32]], axis=0),
            jnp.concatenate([none, none, third, none[0:8]], axis=0),
        ],
        axis=1,
    )[:, 0:192]
    hi, lo = split(wx)
    wx_all[...] = jnp.concatenate([hi, hi, lo], axis=1)

    for copy in early_copies[4:]:
        copy.wait()
    acc[...] = jnp.zeros_like(acc)

    def fold(a):
        out = a[:, 0:128]
        for i in range(1, 6):
            out = out + a[:, 128 * i : 128 * (i + 1)]
        return out

    def rows_of(a):
        return jnp.sum(a, axis=0, keepdims=True)

    lane8 = lanes((8, 768))
    row8 = lax.broadcasted_iota(jnp.int32, (8, 768), 0)
    square = jnp.zeros((8, 768), F32)
    rough = jnp.zeros((8, 768), F32)
    for g in range(6):
        a = [bx[zl, 8 + 8 * g : 16 + 8 * g, IN] for zl in range(2)]
        d = a[0] - a[1]
        rough = rough + d * d
        for zl in range(2):
            square = square + a[zl] * a[zl]
            d = jnp.where(lane8 == 0, 0.0, a[zl] - pltpu.roll(a[zl], 1, 1))
            rough = rough + d * d
            if g > 0:
                d = a[zl] - bx[zl, 7 + 8 * g : 15 + 8 * g, IN]
            else:
                d = jnp.where(row8 == 0, 0.0, a[zl] - pltpu.roll(a[zl], 1, 0))
            rough = rough + d * d
    tile_a[0, 0:1, :] = rows_of(fold(square))
    tile_a[0, 1:2, :] = rows_of(fold(rough))

    lane48 = lanes((TB, 128))

    def rim_copies(i):
        up, down = (r + 63) % 64, (r + 1) % 64
        left, right = (c + 3) % 4, (c + 1) % 4
        used = slice(0, 8) if i == 0 else slice(0, 16)

        def copy(src, dst, d, peer):
            return pltpu.make_async_remote_copy(
                src_ref=src, dst_ref=dst, send_sem=hs_sem.at[i, d], recv_sem=hr_sem.at[i, d],
                device_id=peer, device_id_type=MESH,
            )

        east, west = hs_col.at[i, 0], hs_col.at[i, 1]
        low, high, own = pl.ds(0, 8), pl.ds(56, 8), pl.ds(8, TB)
        return (
            copy(hs_row.at[i, 0, used], hr_row.at[i, 0, used], 0, (down, c)),
            copy(hs_row.at[i, 1, used], hr_row.at[i, 1, used], 1, (up, c)),
            copy(east, hr_col.at[i, 0, own], 2, (r, right)),
            copy(west, hr_col.at[i, 1, own], 3, (r, left)),
            copy(east.at[pl.ds(40, 8)], hr_col.at[i, 0, low], 4, (down, right)),
            copy(east.at[pl.ds(0, 8)], hr_col.at[i, 0, high], 5, (up, right)),
            copy(west.at[pl.ds(40, 8)], hr_col.at[i, 1, low], 6, (down, left)),
            copy(west.at[pl.ds(0, 8)], hr_col.at[i, 1, high], 7, (up, left)),
        )

    def rim_start(i, planes):
        east = west = None
        for j, (f, zl) in enumerate(planes):
            e = f[zl, 8:56, 768:896]
            w = f[zl, 8:56, 128:256]
            if j == 0:
                east, west = e, w
            else:
                east = jnp.where(lane48 < 128 - 3 * j, pltpu.roll(e, 128 - 3 * j, 1), east)
                west = jnp.where(lane48 >= 3 * j, pltpu.roll(w, 3 * j, 1), west)
        hs_col[i, 0] = east
        hs_col[i, 1] = west
        for j, (f, zl) in enumerate(planes):
            hs_row[i, 0, 3 * j : 3 * j + 3, :] = f[zl, 53:56, IN]
            hs_row[i, 1, 3 * j : 3 * j + 3, :] = f[zl, 8:11, IN]
        for copy in rim_copies(i):
            copy.start()

    def rim_wait(i, planes):
        for copy in rim_copies(i):
            copy.wait()
        east = hr_col[i, 0]
        west = hr_col[i, 1]
        for j, (f, zl) in enumerate(planes):
            f[zl, 5:8, IN] = hr_row[i, 0, 3 * j : 3 * j + 3, :]
            f[zl, 56:59, IN] = hr_row[i, 1, 3 * j : 3 * j + 3, :]
            f[zl, :, 0:128] = east if j == 0 else pltpu.roll(east, 3 * j, 1)
            f[zl, :, 896:1024] = west if j == 0 else pltpu.roll(west, 128 - 3 * j, 1)

    source_planes = ((bx, 0), (bx, 1))
    cell_planes = ((ix, 0), (ix, 1), (cc, 0), (cc, 1))

    spot_a = r % 16
    spot_b = y * 4 + c

    def sum_copy(i, stage, j):
        if stage == 0:
            peer = (16 * y + (spot_a + j) % 16, c)
            src, dst = tile_a.at[i], got_a.at[i, spot_a]
        else:
            other = (spot_b + j) % 16
            peer = (16 * (other // 4) + spot_a, other % 4)
            src, dst = tile_b.at[i], got_b.at[i, spot_b]
        return pltpu.make_async_remote_copy(
            src_ref=src, dst_ref=dst, send_sem=ts_sem.at[i, stage], recv_sem=tr_sem.at[i, stage],
            device_id=peer, device_id_type=MESH,
        )

    def sum_start(i, stage):
        @pl.loop(1, 16)
        def _(j):
            sum_copy(i, stage, j).start()

    def sum_wait(i, stage):
        got = got_a if stage == 0 else got_b
        tile = tile_a if stage == 0 else tile_b
        spot = spot_a if stage == 0 else spot_b
        got[i, pl.ds(spot, 1)] = tile[i][None]
        landed = got.at[i, 0:15]
        pltpu.make_async_copy(landed, landed, tr_sem.at[i, stage]).wait()
        total = got[i, 0]
        for j in range(1, 16):
            total = total + got[i, j]
        return total

    def weights_y(k):
        dy, dz = offsets(k, c)
        wh, wl = split(pair_weights(ys_rows, yt_rows, ((y + dy) % 4) * 8 + (z + dz) % 8))
        return jnp.concatenate([wh, wh, wl], axis=1)

    def compute(i):
        steps = [GROUP * i + j for j in range(GROUP)]
        for k in steps:
            fetch(k).wait()
        wy = [weights_y(k) for k in steps]
        cells = [fbuf[k] for k in steps]
        for f in cells:
            for p in range(3):
                acc[p] = acc[p] + jnp.sum(f[p].reshape(8, 8, 128), axis=0)
        outs = []
        for f, w in zip(cells, wy):
            fh, fl = split(f.reshape(192, 128))
            g = dot(wx_all[...], jnp.concatenate([fh, fl, fh], axis=0), ((1,), (0,)))
            gh, gl = split(g)
            outs.append(dot(w, jnp.concatenate([gh, gl, gh], axis=1), ((1,), (1,))))
        for k, out in zip(steps, outs):
            sbuf[2 * k] = out[0:TB]
            sbuf[2 * k + 1] = out[TB : 2 * TB]

    slot = c * 16 + z * 2 + core

    def deliver(src, row, col):
        mine = jnp.logical_and(row == r, col == c)

        @pl.when(mine)
        def _():
            pltpu.make_async_copy(src, rb2.at[slot], rsem2.at[slot]).start()

        @pl.when(jnp.logical_not(mine))
        def _():
            pltpu.make_async_remote_copy(
                src_ref=src, dst_ref=rb2.at[slot], send_sem=ssem2, recv_sem=rsem2.at[slot],
                device_id=(row, col), device_id_type=MESH,
            ).start()

    def send(k):
        dy, dz = offsets(k, c)
        for s in range(2):
            chunk = sbuf.at[2 * k + s]

            @pl.when(dy == 0)
            def _():
                deliver(chunk, 16 * y + (z + dz) % 8 * 2 + s, y)

            @pl.when(dy != 0)
            def _():
                pltpu.make_async_remote_copy(
                    src_ref=chunk, dst_ref=rb1.at[2 * k + s],
                    send_sem=ssem, recv_sem=rsem1.at[2 * k + s],
                    device_id=((r + 16 * dy) % 64, c), device_id_type=MESH,
                ).start()

    def forward(k):
        dy, dz = offsets(k, c)

        @pl.when(dy != 0)
        def _():
            for s in range(2):
                chunk = rb1.at[2 * k + s]
                pltpu.make_async_copy(chunk, chunk, rsem1.at[2 * k + s]).wait()
                deliver(chunk, 16 * y + (z + dz) % 8 * 2 + s, (y - dy + 4) % 4)

    def merge(k):
        cs = (y - k // 2 - c + 32) % 4
        zs = (z - offsets(k, c)[1] + 8) % 8
        for s in range(2):
            block = zs * 2 + s
            place = cs * 16 + block
            got = rb2.at[place]
            pltpu.make_async_copy(got, got, rsem2.at[place]).wait()
            chunk = rb2[place]
            for p in range(3):
                width = TB if p < 2 else 24
                pos = TB * block + (24 * (cs % 2) if p == 2 else 0)
                t0 = pos // 128
                off = pos % 128
                t1 = jnp.minimum(t0 + 1, 5)
                turned = pltpu.roll(chunk, (off + 256 - TB * p) % 128, 1)
                m = (cs // 2) * M + 3 * (cs % 2) + p
                here = pl.ds(pl.multiple_of(t0 * 128, 128), 128)
                inside = jnp.logical_and(lane48 >= off, lane48 < off + width)
                R[m, :, here] = jnp.where(inside, turned, R[m, :, here])
                there = pl.ds(pl.multiple_of(t1 * 128, 128), 128)
                R[m, :, there] = jnp.where(lane48 < off + width - 128, turned, R[m, :, there])

    @pl.loop(0, AHEAD // GROUP)
    def _(i):
        compute(i)

    pl.semaphore_wait(barrier, 81)

    @pl.loop(0, WINDOW)
    def _(k):
        send(k)

    rim_start(0, source_planes)

    @pl.loop(0, NQ + LAG_MERGE)
    def _(it):
        @pl.when(jnp.logical_and(it < NQ - AHEAD, it % GROUP == 0))
        def _():
            compute((it + AHEAD) // GROUP)

        @pl.when(it == NQ - AHEAD)
        def _():
            hf = half.astype(F32)
            for p in range(3):
                v = rows_of(acc[p])
                tile_a[0, 2 + p : 3 + p, :] = v * (1.0 - hf)
                tile_a[0, 5 + p : 6 + p, :] = v * hf
            sum_start(0, 0)

        @pl.when(it < NQ)
        def _():
            forward(it)

        @pl.when(it < NQ - WINDOW)
        def _():
            send(it + WINDOW)

        @pl.when(it == NQ - AHEAD + 8)
        def _():
            tile_b[0] = sum_wait(0, 0)
            sum_start(0, 1)

        @pl.when(it >= LAG_MERGE)
        def _():
            merge(it - LAG_MERGE)

    param = [16.0 / jnp.full((1, 128), table[i].astype(F32)) for i in range(M)]
    param += [jnp.full((1, 128), capacity[i]) for i in range(M)]

    for t in range(6):
        at = slice(128 * t, 128 * (t + 1))
        low = lax.rem(lanes((1, 128)) + 128 * t, TB) < 24
        for zl in range(2):
            m = [R[M * zl + i, :, at] for i in range(M)]
            rest = 1.0 - (m[0] + m[1] + m[3] + m[4])
            m[2], m[5] = jnp.where(low, m[2], rest - m[5]), jnp.where(low, rest - m[2], m[5])
            R[M * zl + 2, :, at] = m[2]
            R[M * zl + 5, :, at] = m[5]
            inverse = m[0] * param[0]
            heat = m[0] * param[M]
            for i in range(1, M):
                inverse = inverse + m[i] * param[i]
                heat = heat + m[i] * param[M + i]
            ix[zl, 8:56, 128 + 128 * t : 256 + 128 * t] = inverse
            cc[zl, 8:56, 128 + 128 * t : 256 + 128 * t] = heat
    rim_start(1, cell_planes)
    rim_wait(0, source_planes)

    param = [a[:, 0:1] for a in param]
    early = jnp.sum(sum_wait(0, 1), axis=1, keepdims=True)
    norm = early[0:1]
    weight = early[2:3]
    mean_c = early[2:3] * param[M]
    mean_i = early[2:3] * param[0]
    for i in range(1, M):
        weight = weight + early[2 + i : 3 + i]
        mean_c = mean_c + early[2 + i : 3 + i] * param[M + i]
        mean_i = mean_i + early[2 + i : 3 + i] * param[i]
    sigma = mean_c / weight + early[1:2] / norm * weight / mean_i
    per = 1.0 / sigma

    def shifted(f, zl, g):
        w = f[zl, 8 * g : 8 * g + 8, :]
        above = f[zl, 8 * g - 1 : 8 * g + 7, :] if g > 0 else pltpu.roll(w, 1, 0)
        below = f[zl, 8 * g + 1 : 8 * g + 9, :] if g < 7 else pltpu.roll(w, 7, 0)
        return w, above, below

    def apply(f, out, groups):
        odd = jnp.zeros((8, 768), F32)
        even = jnp.zeros((8, 768), F32)
        for zl in range(2):
            for g in groups:
                at = slice(8 * g, 8 * g + 8)
                w, above, below = shifted(f, zl, g)
                face_above = fu[zl, at, :]
                v = cc[zl, at, :] * w + fz[at, :] * (w - f[1 - zl, at, :])
                v = v + face_above * (w - above)
                face_below = fu[zl, 8 * g + 1 : 8 * g + 9, :] if g < 7 else pltpu.roll(face_above, 7, 0)
                v = v + face_below * (w - below)
                flow = fl[zl, at, :] * (w - pltpu.roll(w, 1, 1))
                v = v + (flow - pltpu.roll(flow, 1023, 1))
                out[zl, at, :] = v
                if 1 <= g <= 6:
                    w, v = w[:, IN], v[:, IN]
                    odd = odd + w * v
                    even = even + v * v
        return rows_of(fold(odd)), rows_of(fold(even))

    rim_wait(1, cell_planes)
    zero, one = jnp.float32(0.0), jnp.float32(1.0)
    top = jnp.where(r == 0, zero, one)
    bottom = jnp.where(r == 63, zero, one)
    first = jnp.where(c == 0, zero, one)
    last = jnp.where(c == 3, zero, one)
    twice = jnp.broadcast_to(2.0 * per, (8, 1024))
    lane_ext = lanes((8, 1024))
    row_ext = lax.broadcasted_iota(jnp.int32, (8, 1024), 0)
    walls = jnp.where(lane_ext == 128, first, jnp.where(lane_ext == 896, last, one))
    for zl in range(2):
        for g in range(8):
            at = slice(8 * g, 8 * g + 8)
            w = ix[zl, at, :]
            above = ix[zl, 8 * g - 1 : 8 * g + 7, :] if g > 0 else pltpu.roll(w, 1, 0)
            f = twice / (w + above)
            if g in (1, 7):
                f = f * jnp.where(row_ext == 0, top if g == 1 else bottom, one)
            fu[zl, at, :] = f
            fl[zl, at, :] = twice / (w + pltpu.roll(w, 1, 1)) * walls
            if zl == 0:
                fz[at, :] = twice / (w + ix[1, at, :])
            cc[zl, at, :] = cc[zl, at, :] * per - 1.0

    tile_a[1] = jnp.zeros((8, 128), F32)
    s1, s2 = apply(bx, v1, range(8))
    tile_a[1, 0:1, :] = s1
    tile_a[1, 1:2, :] = s2
    s1, s2 = apply(v1, v2, range(8))
    tile_a[1, 2:3, :] = s1
    tile_a[1, 3:4, :] = s2
    s1, s2 = apply(v2, v3, range(1, 7))
    tile_a[1, 4:5, :] = s1
    sum_start(1, 0)
    tile_b[1] = sum_wait(1, 0)
    sum_start(1, 1)
    sums = jnp.sum(sum_wait(1, 1), axis=1, keepdims=True)
    mom = [norm] + [sums[i : i + 1] for i in range(5)]

    def inner(p, q):
        total = None
        for i, pi in enumerate(p):
            for j, qj in enumerate(q):
                term = pi * qj * mom[i + j]
                total = term if total is None else total + term
        return total

    def combine(p, q, s):
        size = max(len(p), len(q))
        out = []
        for i in range(size):
            if i < len(p) and i < len(q):
                out.append(p[i] + s * q[i])
            else:
                out.append(p[i] if i < len(p) else s * q[i])
        return out

    unit = jnp.ones((1, 1), F32)
    x, res, direction, rr = [], [unit], [unit], norm
    for it in range(3):
        n = len(direction)
        applied = [direction[0] * sigma]
        applied += [(direction[i] + direction[i - 1]) * sigma for i in range(1, n)]
        applied += [direction[n - 1] * sigma]
        alpha = rr / inner(direction, applied)
        x = combine(x, direction, alpha)
        res = combine(res, applied, -alpha)
        if it < 2:
            new = inner(res, res)
            direction = combine(res, direction, new / rr)
            rr = new

    for zl in range(2):
        for g in range(6):
            at = slice(8 * g, 8 * g + 8)
            ext = slice(8 + 8 * g, 16 + 8 * g)
            base = [v[zl, ext, IN] for v in (bx, v1, v2, v3)]
            out = x[0] * base[0]
            for i in range(1, 3):
                out = out + x[i] * base[i]
            x_out[zl, at, :] = out
            out = res[0] * base[0]
            for i in range(1, 4):
                out = out + res[i] * base[i]
            r_out[zl, at, :] = out

    sent = sbuf.at[0:48]
    pltpu.make_async_copy(sent, sent, ssem).wait()
    sent = rb2.at[0:63]
    pltpu.make_async_copy(sent, sent, ssem2).wait()
    for i in range(2):
        for stage in range(2):
            sent = got_a.at[i, 0:15]
            pltpu.make_async_copy(sent, sent, ts_sem.at[i, stage]).wait()


def put_out(*refs):
    sem = refs[6]
    copies = [pltpu.make_async_copy(refs[i], refs[3 + i], sem.at[i]) for i in range(3)]
    for copy in copies:
        copy.start()
    for copy in copies:
        copy.wait()


def per_device(
    fractions_source,
    x_source_edges,
    x_target_edges,
    y_source_edges,
    y_target_edges,
    conductivity_table,
    capacity,
    thermal_source_term,
):
    field = jax.ShapeDtypeStruct((2, TB, 768), F32)
    vmem = pl.BlockSpec(memory_space=pltpu.VMEM)
    hbm = pl.BlockSpec(memory_space=pltpu.HBM)
    shapes = (jax.ShapeDtypeStruct((2 * M, TB, 768), F32), field, field)
    ext = VM((2, 64, 1024), F32)
    made = pl.pallas_call(
        kernel,
        out_shape=shapes,
        in_specs=[hbm] * 8,
        out_specs=(vmem, vmem, vmem),
        scratch_shapes=[
            VM((4097,), jnp.int32), VM((3073,), jnp.int32),
            VM((4097,), jnp.int32), VM((3073,), jnp.int32),
            VM((40, 128), F32), VM((32, 128), F32), VM((40, 128), F32), VM((32, 128), F32),
            pltpu.SMEM((M,), jnp.int32), pltpu.SMEM((M,), F32),
            VM((NQ, 3, 64, 128), F32),
            VM((96, 128), F32),
            VM((128, 576), BF16),
            VM((64, TB, 128), F32), VM((64, TB, 128), F32), VM((64, TB, 128), F32),
            ext, ext, ext, ext, ext, ext,
            ext, ext, VM((64, 1024), F32),
            VM((2, 2, 16, 768), F32), VM((2, 2, 16, 768), F32),
            VM((2, 2, TB, 128), F32), VM((2, 2, 64, 128), F32),
            VM((3, 8, 128), F32),
            VM((2, 8, 128), F32), VM((2, 16, 8, 128), F32),
            VM((2, 8, 128), F32), VM((2, 16, 8, 128), F32),
            DMA((7,)), DMA((NQ,)), DMA, DMA((64,)), DMA, DMA((64,)),
            DMA((2, 8)), DMA((2, 8)), DMA((2, 2)), DMA((2, 2)),
        ],
        compiler_params=pltpu.CompilerParams(
            collective_id=0, has_side_effects=True, vmem_limit_bytes=48 * 2**20
        ),
    )(
        *[
            pltpu.with_memory_space_constraint(a, pltpu.HBM)
            for a in (
                fractions_source, x_source_edges, x_target_edges, y_source_edges, y_target_edges,
                conductivity_table, capacity, thermal_source_term,
            )
        ]
    )
    return pl.pallas_call(
        put_out,
        out_shape=shapes,
        in_specs=[pl.BlockSpec(memory_space=pl.ANY)] * 3,
        out_specs=(hbm, hbm, hbm),
        scratch_shapes=[DMA((3,))],
        compiler_params=pltpu.CompilerParams(vmem_limit_bytes=2**20),
    )(*made)


def solution(mesh):
    placed = (P("col", "row", None), P(), P(), P(), P(), P(), P(), P(None, "row", "col"))
    return jax.shard_map(
        per_device,
        mesh=mesh,
        in_specs=placed,
        out_specs=(P(None, "row", "col"), P(None, "row", "col"), P(None, "row", "col")),
        check_vma=False,
    )
```

```python
import jax
import jax.numpy as jnp
from jax import lax
from jax.experimental import pallas as pl
from jax.experimental.pallas import tpu as pltpu
from jax.sharding import PartitionSpec as P

M = 6
TB = 48
NQ = 32
GROUP = 4
AHEAD = 8
WINDOW = 8
LAG_MERGE = 16
MESH = pl.DeviceIdType.MESH
F32 = jnp.float32
BF16 = jnp.bfloat16
VM = pltpu.VMEM
DMA = pltpu.SemaphoreType.DMA
IN = slice(128, 896)


def split(a):
    high = a.astype(BF16)
    return high, (a - high.astype(F32)).astype(BF16)


def dot(a, b, dims):
    return lax.dot_general(a, b, (dims, ((), ())), preferred_element_type=F32)


def offsets(k, c):
    g, s = k // 8, k % 2
    far = (g + 1) % 4
    dz = jnp.where(s == 0, 4 - far, jnp.where(far == 0, 0, 4 + far))
    return (k // 2 + c) % 4, dz


def lanes(shape):
    return lax.broadcasted_iota(jnp.int32, shape, len(shape) - 1)


def kernel(
    frac, xs_edges, xt_edges, ys_edges, yt_edges, table_in, capacity_in, b_ref, R, x_out, r_out,
    xs_line, xt_line, ys_line, yt_line, xs_rows, xt_rows, ys_rows, yt_rows,
    table, capacity, fbuf, wxp, wx_all, sbuf, rb1, rb2, bx, ix, v1, v2, v3, cc,
    fu, fl, fz, hs_row, hr_row, hs_col, hr_col, acc, tile_a, got_a, tile_b, got_b,
    esem, fsem, ssem, rsem1, ssem2, rsem2, hs_sem, hr_sem, ts_sem, tr_sem,
):
    r = lax.axis_index("row")
    c = lax.axis_index("col")
    core = r % 2
    chip = r // 2
    y, z = chip // 8, chip % 8
    half = c % 2

    barrier = pltpu.get_barrier_semaphore()

    def greet(row, col):
        pl.semaphore_signal(barrier, inc=1, device_id=(row, col), device_id_type=MESH)

    @pl.loop(0, 63)
    def _(j):
        j = (j + 31) % 63 + 1
        greet(16 * y + (r + j // 4) % 16, (c + j % 4) % 4)

    @pl.loop(0, 9)
    def _(j):
        greet((r + 16 * (1 + j // 3)) % 64, (c + 1 + j % 3) % 4)

    @pl.loop(1, 4)
    def _(j):
        greet((r + 16 * j) % 64, c)

    for side in (1, 63):
        greet((r + side) % 64, c)
        greet((r + side) % 64, (c + 1) % 4)
        greet((r + side) % 64, (c + 3) % 4)

    lines = ((xs_edges, xs_line), (xt_edges, xt_line), (ys_edges, ys_line), (yt_edges, yt_line))
    early_copies = [pltpu.make_async_copy(a, b, esem.at[i]) for i, (a, b) in enumerate(lines)]
    early_copies.append(pltpu.make_async_copy(b_ref, bx.at[:, 8:56, IN], esem.at[4]))
    early_copies.append(pltpu.make_async_copy(table_in, table, esem.at[5]))
    early_copies.append(pltpu.make_async_copy(capacity_in, capacity, esem.at[6]))
    for copy in early_copies:
        copy.start()

    def fetch(k):
        dy, dz = offsets(k, c)
        q = ((y + dy) % 4) * 8 + (z + dz) % 8
        return pltpu.make_async_copy(
            frac.at[:, :, pl.ds(pl.multiple_of(q * 128, 128), 128)], fbuf.at[k], fsem.at[k]
        )

    @pl.loop(0, NQ)
    def _(k):
        fetch(k).start()

    for i, (line, rows) in enumerate(
        ((xs_line, xs_rows), (xt_line, xt_rows), (ys_line, ys_rows), (yt_line, yt_rows))
    ):
        early_copies[i].wait()
        for q in range(line.shape[0] // 128):
            part = line[128 * q : 128 * (q + 1)]
            rows[q : q + 1, :] = part.astype(F32).reshape(1, 128)
        q = line.shape[0] // 128
        rows[q : q + 1, 0:1] = line[128 * q : 128 * q + 1].astype(F32).reshape(1, 1)

    lane1 = lanes((1, 128))

    def pair_weights(src, tgt, q):
        low = src[pl.ds(q, 1), :]
        high = pltpu.roll(jnp.where(lane1 == 0, src[pl.ds(q + 1, 1), :], low), 127, 1)
        row = 96 * q // 128
        off = 96 * q % 128
        line = jnp.where(lane1 >= off, tgt[pl.ds(row, 1), :], tgt[pl.ds(row + 1, 1), :])
        line = pltpu.roll(line, (128 - off) % 128, 1)
        cols = jnp.broadcast_to(line, (128, 128)).T
        t_low, t_high = cols[0:96], cols[1:97]
        shared = jnp.maximum(jnp.minimum(high, t_high) - jnp.maximum(low, t_low), 0.0)
        return shared / (t_high - t_low)

    wxp[...] = pair_weights(xs_rows, xt_rows, chip)
    wx = wxp[pl.ds(pl.multiple_of(TB * core, 8), TB), :]
    wx = pltpu.roll(wx, 64 * core, 1)
    wxp[0:TB, :] = wx
    third = wxp[pl.ds(pl.multiple_of(24 * half, 8), 24), :]
    none = jnp.zeros((TB, 128), F32)
    wx = jnp.concatenate(
        [
            jnp.concatenate([wx, pltpu.roll(wx, 64, 1), none[0:32]], axis=0),
            jnp.concatenate([none, none, third, none[0:8]], axis=0),
        ],
        axis=1,
    )[:, 0:192]
    hi, lo = split(wx)
    wx_all[...] = jnp.concatenate([hi, hi, lo], axis=1)

    for copy in early_copies[4:]:
        copy.wait()
    acc[...] = jnp.zeros_like(acc)

    def fold(a):
        out = a[:, 0:128]
        for i in range(1, 6):
            out = out + a[:, 128 * i : 128 * (i + 1)]
        return out

    def rows_of(a):
        return jnp.sum(a, axis=0, keepdims=True)

    lane8 = lanes((8, 768))
    row8 = lax.broadcasted_iota(jnp.int32, (8, 768), 0)
    square = jnp.zeros((8, 768), F32)
    rough = jnp.zeros((8, 768), F32)
    for g in range(6):
        a = [bx[zl, 8 + 8 * g : 16 + 8 * g, IN] for zl in range(2)]
        d = a[0] - a[1]
        rough = rough + d * d
        for zl in range(2):
            square = square + a[zl] * a[zl]
            d = jnp.where(lane8 == 0, 0.0, a[zl] - pltpu.roll(a[zl], 1, 1))
            rough = rough + d * d
            if g > 0:
                d = a[zl] - bx[zl, 7 + 8 * g : 15 + 8 * g, IN]
            else:
                d = jnp.where(row8 == 0, 0.0, a[zl] - pltpu.roll(a[zl], 1, 0))
            rough = rough + d * d
    tile_a[0, 0:1, :] = rows_of(fold(square))
    tile_a[0, 1:2, :] = rows_of(fold(rough))

    lane48 = lanes((TB, 128))

    def rim_copies(i):
        up, down = (r + 63) % 64, (r + 1) % 64
        left, right = (c + 3) % 4, (c + 1) % 4
        used = slice(0, 8) if i == 0 else slice(0, 16)

        def copy(src, dst, d, peer):
            return pltpu.make_async_remote_copy(
                src_ref=src, dst_ref=dst, send_sem=hs_sem.at[i, d], recv_sem=hr_sem.at[i, d],
                device_id=peer, device_id_type=MESH,
            )

        east, west = hs_col.at[i, 0], hs_col.at[i, 1]
        low, high, own = pl.ds(0, 8), pl.ds(56, 8), pl.ds(8, TB)
        return (
            copy(hs_row.at[i, 0, used], hr_row.at[i, 0, used], 0, (down, c)),
            copy(hs_row.at[i, 1, used], hr_row.at[i, 1, used], 1, (up, c)),
            copy(east, hr_col.at[i, 0, own], 2, (r, right)),
            copy(west, hr_col.at[i, 1, own], 3, (r, left)),
            copy(east.at[pl.ds(40, 8)], hr_col.at[i, 0, low], 4, (down, right)),
            copy(east.at[pl.ds(0, 8)], hr_col.at[i, 0, high], 5, (up, right)),
            copy(west.at[pl.ds(40, 8)], hr_col.at[i, 1, low], 6, (down, left)),
            copy(west.at[pl.ds(0, 8)], hr_col.at[i, 1, high], 7, (up, left)),
        )

    def rim_start(i, planes):
        east = west = None
        for j, (f, zl) in enumerate(planes):
            e = f[zl, 8:56, 768:896]
            w = f[zl, 8:56, 128:256]
            if j == 0:
                east, west = e, w
            else:
                east = jnp.where(lane48 < 128 - 3 * j, pltpu.roll(e, 128 - 3 * j, 1), east)
                west = jnp.where(lane48 >= 3 * j, pltpu.roll(w, 3 * j, 1), west)
        hs_col[i, 0] = east
        hs_col[i, 1] = west
        for j, (f, zl) in enumerate(planes):
            hs_row[i, 0, 3 * j : 3 * j + 3, :] = f[zl, 53:56, IN]
            hs_row[i, 1, 3 * j : 3 * j + 3, :] = f[zl, 8:11, IN]
        for copy in rim_copies(i):
            copy.start()

    def rim_wait(i, planes):
        for copy in rim_copies(i):
            copy.wait()
        east = hr_col[i, 0]
        west = hr_col[i, 1]
        for j, (f, zl) in enumerate(planes):
            f[zl, 5:8, IN] = hr_row[i, 0, 3 * j : 3 * j + 3, :]
            f[zl, 56:59, IN] = hr_row[i, 1, 3 * j : 3 * j + 3, :]
            f[zl, :, 0:128] = east if j == 0 else pltpu.roll(east, 3 * j, 1)
            f[zl, :, 896:1024] = west if j == 0 else pltpu.roll(west, 128 - 3 * j, 1)

    source_planes = ((bx, 0), (bx, 1))
    cell_planes = ((ix, 0), (ix, 1), (cc, 0), (cc, 1))

    spot_a = r % 16
    spot_b = y * 4 + c

    def sum_copy(i, stage, j):
        if stage == 0:
            peer = (16 * y + (spot_a + j) % 16, c)
            src, dst = tile_a.at[i], got_a.at[i, spot_a]
        else:
            other = (spot_b + j) % 16
            peer = (16 * (other // 4) + spot_a, other % 4)
            src, dst = tile_b.at[i], got_b.at[i, spot_b]
        return pltpu.make_async_remote_copy(
            src_ref=src, dst_ref=dst, send_sem=ts_sem.at[i, stage], recv_sem=tr_sem.at[i, stage],
            device_id=peer, device_id_type=MESH,
        )

    def sum_start(i, stage):
        @pl.loop(0, 15)
        def _(j):
            sum_copy(i, stage, (j + 7) % 15 + 1).start()

    def sum_wait(i, stage):
        got = got_a if stage == 0 else got_b
        tile = tile_a if stage == 0 else tile_b
        spot = spot_a if stage == 0 else spot_b
        got[i, pl.ds(spot, 1)] = tile[i][None]
        landed = got.at[i, 0:15]
        pltpu.make_async_copy(landed, landed, tr_sem.at[i, stage]).wait()
        total = got[i, 0]
        for j in range(1, 16):
            total = total + got[i, j]
        return total

    def weights_y(k):
        dy, dz = offsets(k, c)
        wh, wl = split(pair_weights(ys_rows, yt_rows, ((y + dy) % 4) * 8 + (z + dz) % 8))
        return jnp.concatenate([wh, wh, wl], axis=1)

    def compute(i, early):
        steps = [GROUP * i + j for j in range(GROUP)]
        for k in steps:
            fetch(k).wait()
        wy = [weights_y(k) for k in steps]
        cells = [fbuf[k] for k in steps]
        for f in cells if early else ():
            for p in range(3):
                acc[p] = acc[p] + jnp.sum(f[p].reshape(8, 8, 128), axis=0)
        outs = []
        for f, w in zip(cells, wy):
            fh, fl = split(f.reshape(192, 128))
            g = dot(wx_all[...], jnp.concatenate([fh, fl, fh], axis=0), ((1,), (0,)))
            gh, gl = split(g)
            outs.append(dot(w, jnp.concatenate([gh, gl, gh], axis=1), ((1,), (1,))))
        for k, out in zip(steps, outs):
            sbuf[2 * k] = out[0:TB]
            sbuf[2 * k + 1] = out[TB : 2 * TB]

    slot = c * 16 + z * 2 + core

    def deliver(src, row, col):
        mine = jnp.logical_and(row == r, col == c)

        @pl.when(mine)
        def _():
            pltpu.make_async_copy(src, rb2.at[slot], rsem2.at[slot]).start()

        @pl.when(jnp.logical_not(mine))
        def _():
            pltpu.make_async_remote_copy(
                src_ref=src, dst_ref=rb2.at[slot], send_sem=ssem2, recv_sem=rsem2.at[slot],
                device_id=(row, col), device_id_type=MESH,
            ).start()

    def send(k):
        dy, dz = offsets(k, c)
        for s in range(2):
            chunk = sbuf.at[2 * k + s]

            @pl.when(dy == 0)
            def _():
                deliver(chunk, 16 * y + (z + dz) % 8 * 2 + s, y)

            @pl.when(dy != 0)
            def _():
                pltpu.make_async_remote_copy(
                    src_ref=chunk, dst_ref=rb1.at[2 * k + s],
                    send_sem=ssem, recv_sem=rsem1.at[2 * k + s],
                    device_id=((r + 16 * dy) % 64, c), device_id_type=MESH,
                ).start()

    def forward(k):
        dy, dz = offsets(k, c)

        @pl.when(dy != 0)
        def _():
            for s in range(2):
                chunk = rb1.at[2 * k + s]
                pltpu.make_async_copy(chunk, chunk, rsem1.at[2 * k + s]).wait()
                deliver(chunk, 16 * y + (z + dz) % 8 * 2 + s, (y - dy + 4) % 4)

    def merge(k):
        cs = (y - k // 2 - c + 32) % 4
        zs = (z - offsets(k, c)[1] + 8) % 8
        for s in range(2):
            block = zs * 2 + s
            place = cs * 16 + block
            got = rb2.at[place]
            pltpu.make_async_copy(got, got, rsem2.at[place]).wait()
            chunk = rb2[place]
            for p in range(3):
                width = TB if p < 2 else 24
                pos = TB * block + (24 * (cs % 2) if p == 2 else 0)
                t0 = pos // 128
                off = pos % 128
                t1 = jnp.minimum(t0 + 1, 5)
                turned = pltpu.roll(chunk, (off + 256 - TB * p) % 128, 1)
                m = (cs // 2) * M + 3 * (cs % 2) + p
                here = pl.ds(pl.multiple_of(t0 * 128, 128), 128)
                inside = jnp.logical_and(lane48 >= off, lane48 < off + width)
                R[m, :, here] = jnp.where(inside, turned, R[m, :, here])
                there = pl.ds(pl.multiple_of(t1 * 128, 128), 128)
                R[m, :, there] = jnp.where(lane48 < off + width - 128, turned, R[m, :, there])

    @pl.loop(0, AHEAD // GROUP)
    def _(i):
        compute(i, True)

    hf = half.astype(F32)
    for p in range(3):
        v = rows_of(acc[p])
        tile_a[0, 2 + p : 3 + p, :] = v * (1.0 - hf)
        tile_a[0, 5 + p : 6 + p, :] = v * hf

    pl.semaphore_wait(barrier, 81)
    sum_start(0, 0)

    @pl.loop(0, WINDOW)
    def _(k):
        send(k)

    rim_start(0, source_planes)

    @pl.loop(0, NQ + LAG_MERGE)
    def _(it):
        @pl.when(jnp.logical_and(it < NQ - AHEAD, it % GROUP == 0))
        def _():
            compute((it + AHEAD) // GROUP, False)

        @pl.when(it < NQ)
        def _():
            forward(it)

        @pl.when(it < NQ - WINDOW)
        def _():
            send(it + WINDOW)

        @pl.when(it == 8)
        def _():
            tile_b[0] = sum_wait(0, 0)
            sum_start(0, 1)

        @pl.when(it >= LAG_MERGE)
        def _():
            merge(it - LAG_MERGE)

    param = [16.0 / jnp.full((1, 128), table[i].astype(F32)) for i in range(M)]
    param += [jnp.full((1, 128), capacity[i]) for i in range(M)]

    for t in range(6):
        at = slice(128 * t, 128 * (t + 1))
        low = lax.rem(lanes((1, 128)) + 128 * t, TB) < 24
        for zl in range(2):
            m = [R[M * zl + i, :, at] for i in range(M)]
            rest = 1.0 - (m[0] + m[1] + m[3] + m[4])
            m[2], m[5] = jnp.where(low, m[2], rest - m[5]), jnp.where(low, rest - m[2], m[5])
            R[M * zl + 2, :, at] = m[2]
            R[M * zl + 5, :, at] = m[5]
            inverse = m[0] * param[0]
            heat = m[0] * param[M]
            for i in range(1, M):
                inverse = inverse + m[i] * param[i]
                heat = heat + m[i] * param[M + i]
            ix[zl, 8:56, 128 + 128 * t : 256 + 128 * t] = inverse
            cc[zl, 8:56, 128 + 128 * t : 256 + 128 * t] = heat
    rim_start(1, cell_planes)
    rim_wait(0, source_planes)

    param = [a[:, 0:1] for a in param]
    early = jnp.sum(sum_wait(0, 1), axis=1, keepdims=True)
    norm = early[0:1]
    weight = early[2:3]
    mean_c = early[2:3] * param[M]
    mean_i = early[2:3] * param[0]
    for i in range(1, M):
        weight = weight + early[2 + i : 3 + i]
        mean_c = mean_c + early[2 + i : 3 + i] * param[M + i]
        mean_i = mean_i + early[2 + i : 3 + i] * param[i]
    sigma = mean_c / weight + early[1:2] / norm * weight / mean_i
    per = 1.0 / sigma

    def shifted(f, zl, g):
        w = f[zl, 8 * g : 8 * g + 8, :]
        above = f[zl, 8 * g - 1 : 8 * g + 7, :] if g > 0 else pltpu.roll(w, 1, 0)
        below = f[zl, 8 * g + 1 : 8 * g + 9, :] if g < 7 else pltpu.roll(w, 7, 0)
        return w, above, below

    def apply(f, out, groups):
        odd = jnp.zeros((8, 768), F32)
        even = jnp.zeros((8, 768), F32)
        for zl in range(2):
            for g in groups:
                at = slice(8 * g, 8 * g + 8)
                w, above, below = shifted(f, zl, g)
                face_above = fu[zl, at, :]
                v = cc[zl, at, :] * w + fz[at, :] * (w - f[1 - zl, at, :])
                v = v + face_above * (w - above)
                face_below = fu[zl, 8 * g + 1 : 8 * g + 9, :] if g < 7 else pltpu.roll(face_above, 7, 0)
                v = v + face_below * (w - below)
                flow = fl[zl, at, :] * (w - pltpu.roll(w, 1, 1))
                v = v + (flow - pltpu.roll(flow, 1023, 1))
                out[zl, at, :] = v
                if 1 <= g <= 6:
                    w, v = w[:, IN], v[:, IN]
                    odd = odd + w * v
                    even = even + v * v
        return rows_of(fold(odd)), rows_of(fold(even))

    rim_wait(1, cell_planes)
    zero, one = jnp.float32(0.0), jnp.float32(1.0)
    top = jnp.where(r == 0, zero, one)
    bottom = jnp.where(r == 63, zero, one)
    first = jnp.where(c == 0, zero, one)
    last = jnp.where(c == 3, zero, one)
    twice = jnp.broadcast_to(2.0 * per, (8, 1024))
    lane_ext = lanes((8, 1024))
    row_ext = lax.broadcasted_iota(jnp.int32, (8, 1024), 0)
    walls = jnp.where(lane_ext == 128, first, jnp.where(lane_ext == 896, last, one))
    for zl in range(2):
        for g in range(8):
            at = slice(8 * g, 8 * g + 8)
            w = ix[zl, at, :]
            above = ix[zl, 8 * g - 1 : 8 * g + 7, :] if g > 0 else pltpu.roll(w, 1, 0)
            f = twice / (w + above)
            if g in (1, 7):
                f = f * jnp.where(row_ext == 0, top if g == 1 else bottom, one)
            fu[zl, at, :] = f
            fl[zl, at, :] = twice / (w + pltpu.roll(w, 1, 1)) * walls
            if zl == 0:
                fz[at, :] = twice / (w + ix[1, at, :])
            cc[zl, at, :] = cc[zl, at, :] * per - 1.0

    tile_a[1] = jnp.zeros((8, 128), F32)
    s1, s2 = apply(bx, v1, range(8))
    tile_a[1, 0:1, :] = s1
    tile_a[1, 1:2, :] = s2
    s1, s2 = apply(v1, v2, range(8))
    tile_a[1, 2:3, :] = s1
    tile_a[1, 3:4, :] = s2
    s1, s2 = apply(v2, v3, range(1, 7))
    tile_a[1, 4:5, :] = s1
    sum_start(1, 0)
    tile_b[1] = sum_wait(1, 0)
    sum_start(1, 1)
    sums = jnp.sum(sum_wait(1, 1), axis=1, keepdims=True)
    mom = [norm] + [sums[i : i + 1] for i in range(5)]

    def inner(p, q):
        total = None
        for i, pi in enumerate(p):
            for j, qj in enumerate(q):
                term = pi * qj * mom[i + j]
                total = term if total is None else total + term
        return total

    def combine(p, q, s):
        size = max(len(p), len(q))
        out = []
        for i in range(size):
            if i < len(p) and i < len(q):
                out.append(p[i] + s * q[i])
            else:
                out.append(p[i] if i < len(p) else s * q[i])
        return out

    unit = jnp.ones((1, 1), F32)
    x, res, direction, rr = [], [unit], [unit], norm
    for it in range(3):
        n = len(direction)
        applied = [direction[0] * sigma]
        applied += [(direction[i] + direction[i - 1]) * sigma for i in range(1, n)]
        applied += [direction[n - 1] * sigma]
        alpha = rr / inner(direction, applied)
        x = combine(x, direction, alpha)
        res = combine(res, applied, -alpha)
        if it < 2:
            new = inner(res, res)
            direction = combine(res, direction, new / rr)
            rr = new

    for zl in range(2):
        for g in range(6):
            at = slice(8 * g, 8 * g + 8)
            ext = slice(8 + 8 * g, 16 + 8 * g)
            base = [v[zl, ext, IN] for v in (bx, v1, v2, v3)]
            out = x[0] * base[0]
            for i in range(1, 3):
                out = out + x[i] * base[i]
            x_out[zl, at, :] = out
            out = res[0] * base[0]
            for i in range(1, 4):
                out = out + res[i] * base[i]
            r_out[zl, at, :] = out

    sent = sbuf.at[0:48]
    pltpu.make_async_copy(sent, sent, ssem).wait()
    sent = rb2.at[0:63]
    pltpu.make_async_copy(sent, sent, ssem2).wait()
    for i in range(2):
        for stage in range(2):
            sent = got_a.at[i, 0:15]
            pltpu.make_async_copy(sent, sent, ts_sem.at[i, stage]).wait()


def put_out(*refs):
    sem = refs[6]
    copies = [pltpu.make_async_copy(refs[i], refs[3 + i], sem.at[i]) for i in range(3)]
    for copy in copies:
        copy.start()
    for copy in copies:
        copy.wait()


def per_device(
    fractions_source,
    x_source_edges,
    x_target_edges,
    y_source_edges,
    y_target_edges,
    conductivity_table,
    capacity,
    thermal_source_term,
):
    field = jax.ShapeDtypeStruct((2, TB, 768), F32)
    vmem = pl.BlockSpec(memory_space=pltpu.VMEM)
    hbm = pl.BlockSpec(memory_space=pltpu.HBM)
    shapes = (jax.ShapeDtypeStruct((2 * M, TB, 768), F32), field, field)
    ext = VM((2, 64, 1024), F32)
    made = pl.pallas_call(
        kernel,
        out_shape=shapes,
        in_specs=[hbm] * 8,
        out_specs=(vmem, vmem, vmem),
        scratch_shapes=[
            VM((4097,), jnp.int32), VM((3073,), jnp.int32),
            VM((4097,), jnp.int32), VM((3073,), jnp.int32),
            VM((40, 128), F32), VM((32, 128), F32), VM((40, 128), F32), VM((32, 128), F32),
            pltpu.SMEM((M,), jnp.int32), pltpu.SMEM((M,), F32),
            VM((NQ, 3, 64, 128), F32),
            VM((96, 128), F32),
            VM((128, 576), BF16),
            VM((64, TB, 128), F32), VM((64, TB, 128), F32), VM((64, TB, 128), F32),
            ext, ext, ext, ext, ext, ext,
            ext, ext, VM((64, 1024), F32),
            VM((2, 2, 16, 768), F32), VM((2, 2, 16, 768), F32),
            VM((2, 2, TB, 128), F32), VM((2, 2, 64, 128), F32),
            VM((3, 8, 128), F32),
            VM((2, 8, 128), F32), VM((2, 16, 8, 128), F32),
            VM((2, 8, 128), F32), VM((2, 16, 8, 128), F32),
            DMA((7,)), DMA((NQ,)), DMA, DMA((64,)), DMA, DMA((64,)),
            DMA((2, 8)), DMA((2, 8)), DMA((2, 2)), DMA((2, 2)),
        ],
        compiler_params=pltpu.CompilerParams(
            collective_id=0, has_side_effects=True, vmem_limit_bytes=48 * 2**20
        ),
    )(
        *[
            pltpu.with_memory_space_constraint(a, pltpu.HBM)
            for a in (
                fractions_source, x_source_edges, x_target_edges, y_source_edges, y_target_edges,
                conductivity_table, capacity, thermal_source_term,
            )
        ]
    )
    return pl.pallas_call(
        put_out,
        out_shape=shapes,
        in_specs=[pl.BlockSpec(memory_space=pl.ANY)] * 3,
        out_specs=(hbm, hbm, hbm),
        scratch_shapes=[DMA((3,))],
        compiler_params=pltpu.CompilerParams(vmem_limit_bytes=2**20),
    )(*made)


def solution(mesh):
    placed = (P("col", "row", None), P(), P(), P(), P(), P(), P(), P(None, "row", "col"))
    return jax.shard_map(
        per_device,
        mesh=mesh,
        in_specs=placed,
        out_specs=(P(None, "row", "col"), P(None, "row", "col"), P(None, "row", "col")),
        check_vma=False,
    )
```
